32 devices in a mesh: row: 8 (over y, x, core), col: 4 (over z).
Axes of the slice: x: 2, y: 2, z: 4, core: 2. Of those that a mesh axis runs over, the one named last changes fastest.
Arguments:
- diag_block: float32 [512, 512], P('row', 'col'), may hold values from 0 to 2.5, as said below
- panel_below: float32 [24576, 512], P('row', 'col'), may hold values from -1.8 to 1.8
- trailing: float32 [24576, 6144], P('row', 'col'), may hold values from -6 to 6
Outputs:
- diag_factor: float32 [512, 512], P('row', 'col')
- panel_factor: float32 [24576, 512], P('row', 'col')
- new_trailing: float32 [24576, 6144], P('row', 'col')
The draws below stay inside these ranges and needn't reach their ends.
Inputs may be any that keep to these rules, and one draw needn't show every extreme that they name: `diag_block`: taken to matrix order in both dimensions, the block is symmetric with all eigenvalues 0.5 or more.
All inputs are finite; a program needn't handle non-finite values.
Results may differ from the reference program's by a relative error of at most 0.00015.
Values sent between devices are 32-bit elements; how exact they have to be, the bound alone decides.
A program may use at most 128 MiB of HBM per device.

```python
import jax
import jax.numpy as jnp
from jax import lax

NB = 512
TC = 6144
BELOW = 24576
N_ROW = 8
N_COL = 4


def draw_diag_block(key, part):
    key_points, key_ridge = jax.random.split(key)
    points = jax.random.uniform(key_points, (NB, 3), jnp.float32, 0.0, 1.0)
    ridge = jax.random.uniform(key_ridge, (NB,), jnp.float32, 0.5, 1.5)
    index = jnp.arange(NB, dtype=jnp.int32)
    rows_block = NB // N_ROW
    cols_block = NB // N_COL
    row_map = index % rows_block * N_ROW + index // rows_block
    col_map = index % cols_block * N_COL + index // cols_block
    row_points = points[row_map]
    col_points = points[col_map]
    distance = jnp.zeros((NB, NB), jnp.float32)
    for coord in range(3):
        gap = row_points[:, coord][:, None] - col_points[:, coord][None, :]
        distance = distance + gap * gap
    length_scale = 0.6 / NB ** (1.0 / 3.0)
    kernel = jnp.exp(-distance / (2.0 * length_scale * length_scale))
    same = row_map[:, None] == col_map[None, :]
    kernel = kernel + jnp.where(same, ridge[row_map][:, None], 0.0)
    return kernel.astype(jnp.float32)


def level_of(key, dims, pieces, least, top_value):
    level = 1.0
    for position, blocks in pieces:
        heights = jax.random.uniform(jax.random.fold_in(jax.random.fold_in(key, 6), position), (blocks,), jnp.float32, least / len(pieces), top_value / len(pieces))
        level = level * jnp.repeat(jnp.exp(heights), dims[position] // blocks).reshape((-1,) + (1,) * (len(dims) - 1 - position))
    return level


def gaussian(stream_key, dims, width, reach, cuts=(), kind=jnp.bfloat16):
    level = level_of(stream_key, dims, cuts, -0.22, 0.18) if cuts else 1.0
    values = jax.random.normal(stream_key, dims, jnp.float32) * width * level
    return jnp.minimum(jnp.maximum(values, -reach), reach).astype(kind)


def setup_inputs(seed: int = 0) -> dict:
    arg_keys = jax.random.split(jax.random.key(seed), 4)
    diag_block = draw_diag_block(jax.random.fold_in(arg_keys[3], 71), 0)
    panel_below = gaussian(arg_keys[1], (BELOW, NB), 0.3, 1.8, ((0, 8), (1, 4)), jnp.float32)
    trailing = gaussian(arg_keys[2], (BELOW, TC), 1.0, 6.0, ((0, 8), (1, 4)), jnp.float32)
    return {"diag_block": diag_block, "panel_below": panel_below, "trailing": trailing}


def to_matrix(array, parts, axis):
    moved = jnp.moveaxis(array, axis, 0)
    length = moved.shape[0]
    shaped = moved.reshape((parts, length // parts) + moved.shape[1:])
    shaped = jnp.swapaxes(shaped, 0, 1).reshape(moved.shape)
    return jnp.moveaxis(shaped, 0, axis)

def to_storage(array, parts, axis):
    moved = jnp.moveaxis(array, axis, 0)
    length = moved.shape[0]
    shaped = moved.reshape((length // parts, parts) + moved.shape[1:])
    shaped = jnp.swapaxes(shaped, 0, 1).reshape(moved.shape)
    return jnp.moveaxis(shaped, 0, axis)

def reference(diag_block, panel_below, trailing):
    diag_matrix = to_matrix(to_matrix(diag_block, N_ROW, 0), N_COL, 1)
    factor = jnp.linalg.cholesky(diag_matrix)
    diag_factor = to_storage(to_storage(factor, N_ROW, 0), N_COL, 1)
    identity = jnp.eye(NB, dtype=jnp.float32)
    inverse = lax.linalg.triangular_solve(factor, identity, left_side=True, lower=True)
    panel_matrix = to_matrix(panel_below, N_COL, 1)
    solved = jnp.dot(panel_matrix.astype(jnp.float32), inverse.T.astype(jnp.float32), precision=lax.Precision.HIGHEST, preferred_element_type=jnp.float32)
    panel_factor = to_storage(solved, N_COL, 1)
    solved_matrix = to_matrix(solved, N_ROW, 0)
    top_store = to_storage(solved_matrix[:TC], N_COL, 0)
    update = jnp.dot(solved.astype(jnp.float32), top_store.T.astype(jnp.float32), precision=lax.Precision.HIGHEST, preferred_element_type=jnp.float32)
    new_trailing = trailing - update
    return (diag_factor, panel_factor, new_trailing)
```

```python
import functools

import jax
import jax.numpy as jnp
from jax import lax
from jax.experimental import pallas as pl
from jax.experimental.pallas import tpu as pltpu
from jax.sharding import PartitionSpec as P

BLOCK = 128
TILE = 8


def full_dot(left, right, dims):
    return lax.dot_general(
        left, right, (dims, ((), ())), precision=lax.Precision.HIGHEST, preferred_element_type=jnp.float32
    )


def one_hot_dot(value, move, pieces):
    total = None
    rest = value
    for _ in range(pieces):
        piece = rest.astype(jnp.bfloat16)
        rest = rest - piece.astype(jnp.float32)
        part = lax.dot_general(move, piece, (((1,), (0,)), ((), ())), preferred_element_type=jnp.float32)
        total = part if total is None else total + part
    return total


def eliminate(s_ref, r_ref, base):
    count = BLOCK // TILE
    shape = (TILE, BLOCK)
    lane = lax.broadcasted_iota(jnp.int32, shape, 1)
    tiles = [s_ref[base + t * TILE : base + (t + 1) * TILE, base : base + BLOCK] for t in range(count)]
    for p in range(count):
        first = p * TILE
        own = tiles[p]
        rows = [jnp.broadcast_to(own[j : j + 1, :], shape) for j in range(TILE)]
        a = [
            [jnp.broadcast_to(rows[i][:, first + j : first + j + 1], shape) for j in range(i + 1)]
            for i in range(TILE)
        ]
        cols = {
            t: [jnp.broadcast_to(tiles[t][:, first + j : first + j + 1], shape) for j in range(TILE)]
            for t in range(p + 1, count)
        }
        for k in range(TILE):
            scale = lax.rsqrt(a[k][k])
            low = [a[i][k] * scale for i in range(k + 1, TILE)]
            row = rows[k] * scale
            r_ref[first + k : first + k + 1, :] = row[0:1, :]
            used = row + jnp.where(lane == first + k, scale, 0.0)
            for i in range(k + 1, TILE):
                rows[i] = rows[i] - low[i - k - 1] * used
                for j in range(k + 1, i + 1):
                    a[i][j] = a[i][j] - low[i - k - 1] * low[j - k - 1]
            for t in range(p + 1, count):
                col = cols[t][k] * scale
                tiles[t] = tiles[t] - col * used
                for j in range(k + 1, TILE):
                    cols[t][j] = cols[t][j] - col * low[j - k - 1]


def split(value):
    high = value.astype(jnp.bfloat16)
    return high, (value - high.astype(jnp.float32)).astype(jnp.bfloat16)


def split_rows(value):
    high, low = split(value)
    return jnp.concatenate([high, high, low], axis=0)


def split_dot(left, right_parts):
    high, low = split(left)
    return lax.dot_general(
        jnp.concatenate([high, low, high], axis=1),
        right_parts,
        (((1,), (0,)), ((), ())),
        preferred_element_type=jnp.float32,
    )


def gather_kernel(row_count, col_count, d_ref, p_ref, g_ref, fwd_ref, bwd_ref, mine_ref, *sems):
    own_sem, mine_send, mine_recv, col_send, col_recv, row_send, row_recv, line_send, line_recv = sems
    r = lax.axis_index("row")
    c = lax.axis_index("col")
    mesh_id = pl.DeviceIdType.MESH
    along_col = [(r, lax.rem(c + d, col_count)) for d in range(1, col_count)]
    along_row = [(lax.rem(r + d, row_count), c) for d in range(1, row_count)]
    q = lax.rem(r, col_count)
    swap = (r - q + c, q)
    barrier = pltpu.get_barrier_semaphore()
    for peer in along_col + along_row:
        pl.semaphore_signal(barrier, inc=1, device_id=peer, device_id_type=mesh_id)

    @pl.when(q != c)
    def _():
        pl.semaphore_signal(barrier, inc=1, device_id=swap, device_id_type=mesh_id)
        pl.semaphore_wait(barrier, row_count + col_count - 1)

    @pl.when(q == c)
    def _():
        pl.semaphore_wait(barrier, row_count + col_count - 2)

    own = pltpu.make_async_copy(d_ref, g_ref.at[r, c], own_sem)
    across = [
        pltpu.make_async_remote_copy(
            src_ref=d_ref, dst_ref=g_ref.at[r, c], send_sem=col_send.at[i], recv_sem=col_recv.at[i],
            device_id=peer, device_id_type=mesh_id,
        )
        for i, peer in enumerate(along_col)
    ]
    for copy in [own] + across:
        copy.start()
    top = p_ref.at[pl.ds(0, mine_ref.shape[0])]
    mine = pltpu.make_async_remote_copy(
        src_ref=top, dst_ref=mine_ref, send_sem=mine_send, recv_sem=mine_recv, device_id=swap, device_id_type=mesh_id
    )
    keep = pltpu.make_async_copy(top, mine_ref, mine_recv)
    head = p_ref.at[pl.ds(0, fwd_ref.shape[0])]
    fwd = pltpu.make_async_remote_copy(
        src_ref=head, dst_ref=fwd_ref, send_sem=line_send.at[0], recv_sem=line_recv.at[0],
        device_id=(r, c + 1), device_id_type=mesh_id,
    )
    bwd = pltpu.make_async_remote_copy(
        src_ref=head, dst_ref=bwd_ref, send_sem=line_send.at[1], recv_sem=line_recv.at[1],
        device_id=(r, c - 1), device_id_type=mesh_id,
    )

    @pl.when(q != c)
    def _():
        mine.start()

    @pl.when(q == c)
    def _():
        keep.start()

    @pl.when(c < col_count - 1)
    def _():
        fwd.start()

    @pl.when(c > 0)
    def _():
        bwd.start()

    for copy in [own] + across:
        copy.wait()
    copies = [
        pltpu.make_async_remote_copy(
            src_ref=g_ref.at[r], dst_ref=g_ref.at[r], send_sem=row_send.at[i], recv_sem=row_recv.at[i],
            device_id=peer, device_id_type=mesh_id,
        )
        for i, peer in enumerate(along_row)
    ]
    for copy in copies:
        copy.start()
    for copy in copies:
        copy.wait()

    @pl.when(q != c)
    def _():
        mine.wait()

    @pl.when(q == c)
    def _():
        keep.wait()

    @pl.when(c < col_count - 1)
    def _():
        fwd.wait_send()
        bwd.wait_recv()

    @pl.when(c > 0)
    def _():
        bwd.wait_send()
        fwd.wait_recv()


def gather_blocks(block, panel, head, top_length, row_count, col_count):
    dma = pltpu.SemaphoreType.DMA
    lanes = panel.shape[1]
    line = jax.ShapeDtypeStruct((head, lanes), panel.dtype)
    return pl.pallas_call(
        functools.partial(gather_kernel, row_count, col_count),
        out_shape=(
            jax.ShapeDtypeStruct((row_count, col_count) + block.shape, block.dtype),
            line,
            line,
            jax.ShapeDtypeStruct((top_length, lanes), panel.dtype),
        ),
        in_specs=[pl.BlockSpec(memory_space=pltpu.VMEM), pl.BlockSpec(memory_space=pl.ANY)],
        out_specs=(pl.BlockSpec(memory_space=pltpu.VMEM),) + (pl.BlockSpec(memory_space=pl.ANY),) * 3,
        scratch_shapes=[
            dma, dma, dma, dma((col_count - 1,)), dma((col_count - 1,)), dma((row_count - 1,)), dma((row_count - 1,)),
            dma((2,)), dma((2,)),
        ],
        compiler_params=pltpu.CompilerParams(collective_id=0, has_side_effects=True),
    )(block, panel)


def chol_kernel(row_count, col_count, a_ref, f_ref, q_ref, e_ref, s_ref, l_ref, x_ref, r_ref):
    width = s_ref.shape[0]
    col = lax.axis_index("col")
    per = width // col_count
    rows_dev = width // row_count
    for r in range(row_count):
        for z in range(col_count):
            s_ref[r * rows_dev : (r + 1) * rows_dev, z * per : (z + 1) * per] = a_ref[r, z]
    natural = lax.broadcasted_iota(jnp.int32, (width, width), 0)
    store = lax.broadcasted_iota(jnp.int32, (width, width), 1)
    from_rows = jnp.where(natural == (store % rows_dev) * row_count + store // rows_dev, 1.0, 0.0).astype(jnp.bfloat16)
    from_cols = jnp.where(natural == (store % per) * col_count + store // per, 1.0, 0.0)
    x_ref[...] = one_hot_dot(s_ref[...], from_rows, 3)
    s_ref[...] = one_hot_dot(x_ref[...].T, from_cols.astype(jnp.bfloat16), 3)
    l_ref[...] = jnp.zeros_like(l_ref)
    x_ref[...] = jnp.zeros_like(x_ref)
    up = lax.broadcasted_iota(jnp.int32, (BLOCK, BLOCK), 0)
    across = lax.broadcasted_iota(jnp.int32, (BLOCK, BLOCK), 1)
    for base in range(0, width, BLOCK):
        end = base + BLOCK
        eliminate(s_ref, r_ref, base)
        both = r_ref[...]
        l_ref[base:end, base:end] = jnp.where(up >= across, both.T, 0.0)
        inv = jnp.where(up > across, both, 0.0) + jnp.where(up == across, 1.0 / both, 0.0)
        x_ref[base:end, base:end] = inv
        if base:
            x_ref[base:end, :base] = -full_dot(
                inv, full_dot(l_ref[base:end, :base], x_ref[:base, :base], ((1,), (0,))), ((1,), (0,))
            )
        if end < width:
            below = full_dot(s_ref[end:, base:end], inv, ((1,), (1,)))
            l_ref[end:, base:end] = below
            s_ref[end:, end:] = s_ref[end:, end:] - full_dot(below, below, ((1,), (1,)))
    r = lax.axis_index("row")
    c = col
    i0 = lax.broadcasted_iota(jnp.int32, (rows_dev, width), 0)
    i1 = lax.broadcasted_iota(jnp.int32, (rows_dev, width), 1)
    pick_rows = jnp.where(i1 == i0 * row_count + r, 1.0, 0.0)
    j0 = lax.broadcasted_iota(jnp.int32, (per, width), 0)
    j1 = lax.broadcasted_iota(jnp.int32, (per, width), 1)
    pick_cols = jnp.where(j1 == j0 * col_count + c, 1.0, 0.0)
    f_ref[...] = full_dot(full_dot(pick_rows, l_ref[...], ((1,), (0,))), pick_cols, ((1,), (1,)))
    turn = lax.rem(c - store // per + col_count, col_count)
    turned = jnp.where(natural == (store % per) * col_count + turn, 1.0, 0.0)
    l_ref[...] = full_dot(x_ref[...], turned, ((1,), (0,)))
    s_ref[...] = full_dot(x_ref[...], from_cols, ((1,), (0,)))
    e_ref[...] = split_rows(full_dot(l_ref[...], pick_cols, ((0,), (1,))))
    q_ref[...] = split_rows(full_dot(s_ref[...], l_ref[...], ((0,), (0,))))


def factorize(blocks, row_count, col_count):
    width = blocks.shape[0] * blocks.shape[2]
    tripled = jax.ShapeDtypeStruct((3 * width, width), jnp.bfloat16)
    return pl.pallas_call(
        functools.partial(chol_kernel, row_count, col_count),
        out_shape=(
            jax.ShapeDtypeStruct((width // row_count, width // col_count), jnp.float32),
            tripled,
            jax.ShapeDtypeStruct((3 * width, width // col_count), jnp.bfloat16),
        ),
        scratch_shapes=[pltpu.VMEM((width, width), jnp.float32)] * 3 + [pltpu.VMEM((BLOCK, BLOCK), jnp.float32)],
        cost_estimate=pl.CostEstimate(flops=28 * width**3 * 8, bytes_accessed=9 * width**2 * 4, transcendentals=0),
        compiler_params=pltpu.CompilerParams(vmem_limit_bytes=32 * 1024 * 1024),
    )(blocks)


def top_kernel(col_count, q_ref, *refs):
    o_ref, t_ref, g_ref = refs[-3:]
    groups, length, _ = g_ref.shape
    r = lax.axis_index("row")
    for d in range(groups):
        g_ref[lax.rem(r + d, groups)] = refs[d][...]
    owners = groups // col_count
    width = q_ref.shape[1]
    for h in range(owners):
        left = jnp.concatenate([g_ref[h * col_count + z] for z in range(col_count)], axis=1)
        solved = split_dot(left, q_ref[...])
        for b in range(width // BLOCK):
            t_ref[b, pl.ds(h, length, stride=owners), :] = solved[:, b * BLOCK : (b + 1) * BLOCK]
    for b in range(width // BLOCK):
        high, low = split(t_ref[b].T)
        at = b * BLOCK
        o_ref[at : at + BLOCK, :] = high
        o_ref[width + at : width + at + BLOCK, :] = high
        o_ref[2 * width + at : 2 * width + at + BLOCK, :] = low


def solve_top(pieces, q_parts, col_count):
    groups = len(pieces)
    length, lanes = pieces[0].shape
    width = q_parts.shape[1]
    columns = groups // col_count * length
    return pl.pallas_call(
        functools.partial(top_kernel, col_count),
        out_shape=jax.ShapeDtypeStruct((3 * width, columns), jnp.bfloat16),
        scratch_shapes=[pltpu.VMEM((width // BLOCK, columns, BLOCK), jnp.float32), pltpu.VMEM((groups, length, lanes), jnp.float32)],
        cost_estimate=pl.CostEstimate(flops=6 * width * width * columns, bytes_accessed=16 * width * columns, transcendentals=0),
        compiler_params=pltpu.CompilerParams(vmem_limit_bytes=36 * 1024 * 1024),
    )(q_parts, *pieces)


def update_kernel(count, *refs):
    pieces = [ref[...] for ref in refs[:count]]
    relay, e_ref, t_ref, c_ref = refs[count : count + 4]
    f_ref, n_ref = refs[-2:]
    c = lax.axis_index("col")
    pieces[1] = jnp.where(c == 0, relay[...], pieces[1])
    pieces[-1] = jnp.where(c == count - 1, relay[...], pieces[-1])
    high, low = split(jnp.concatenate(pieces, axis=1))
    left = jnp.concatenate([high, low, high], axis=1)
    dims = (((1,), (0,)), ((), ()))
    f_ref[...] = lax.dot_general(left, e_ref[...], dims, preferred_element_type=jnp.float32)
    n_ref[...] = c_ref[...] - lax.dot_general(left, t_ref[...], dims, preferred_element_type=jnp.float32)


def update_rows(panel, others, relay, e_parts, top_parts, trailing, offset, previous):
    length, lanes = relay.shape
    rows, columns = trailing.shape
    tile = 256
    first = offset // tile
    count = len(others) + 1
    fixed = lambda a: pl.BlockSpec(a.shape, lambda i: (0, 0), pipeline_mode=pl.Buffered(1))
    strip = lambda n: pl.BlockSpec((tile, n), lambda i: (first + i, 0))
    part = pl.BlockSpec((tile, lanes), lambda i: (i, 0))
    flops = 2 * length * top_parts.shape[0] * (columns + e_parts.shape[1])
    return pl.pallas_call(
        functools.partial(update_kernel, count),
        grid=(length // tile,),
        out_shape=(
            jax.ShapeDtypeStruct((rows, lanes), jnp.float32),
            jax.ShapeDtypeStruct((rows, columns), jnp.float32),
        ),
        in_specs=[strip(lanes)] + [part] * count + [fixed(e_parts), fixed(top_parts), strip(columns)]
        + [pl.BlockSpec(memory_space=pl.ANY)] * len(previous),
        out_specs=(strip(lanes), strip(columns)),
        input_output_aliases={count + 4 + i: i for i in range(len(previous))},
        cost_estimate=pl.CostEstimate(flops=flops, bytes_accessed=length * columns * 8, transcendentals=0),
        compiler_params=pltpu.CompilerParams(vmem_limit_bytes=40 * 1024 * 1024),
    )(panel, *others, relay, e_parts, top_parts, trailing, *previous)


def shift(value, d, count):
    pairs = [(i, (i + d) % count) for i in range(count)]
    return lax.ppermute(value, "col", [p for p in pairs if abs(p[0] - p[1]) < count - 1])


def relay_ends(held, count):
    value = held[2]
    if count != 4:
        value = jnp.where(lax.axis_index("col") == 1, held[2], held[count - 2])
    return lax.ppermute(value, "col", [(1, 0), (count - 2, count - 1)])


def shards(diag_block, panel_below, trailing):
    row_count = lax.axis_size("row")
    n = lax.axis_size("col")
    top_length = trailing.shape[1] // (row_count // n)
    rows = panel_below.shape[0]
    cuts = (0, rows // 3, 3 * rows // 4, rows)
    spans = list(zip(cuts, cuts[1:]))
    blocks, fwd, bwd, mine = gather_blocks(diag_block, panel_below, cuts[1], top_length, row_count, n)
    blocks, mine, panel = lax.optimization_barrier((blocks, mine, panel_below))
    own = [panel[a:b] for a, b in spans]
    held = [{1: fwd, n - 1: bwd}, {}, {}]
    pieces = [mine]
    for d in range(2, n - 1):
        held[0][d] = shift(own[0], d, n)
    for d in range(1, row_count):
        pieces.append(lax.ppermute(mine, "row", [((i + d) % row_count, i) for i in range(row_count)]))
    for d in (1, n - 1):
        held[1][d] = shift(own[1], d, n)
    diag_factor, q_parts, e_parts = factorize(blocks, row_count, n)
    relays = [relay_ends(held[0], n)]
    for d in range(2, n - 1):
        held[1][d] = shift(own[1], d, n)
    for d in list(range(2, n - 1)) + [1, n - 1]:
        held[2][d] = shift(own[2], d, n)
    top_parts = solve_top(pieces, q_parts, n)
    for k in (1, 2):
        relays.append(relay_ends(held[k], n))
    outs = ()
    for (start, _), h, relay in zip(spans, held, relays):
        others = [h[d] for d in range(1, n)]
        outs = update_rows(panel_below, others, relay, e_parts, top_parts, trailing, start, outs)
    return (diag_factor, *outs)


def solution(mesh):
    in_specs = (P("row", "col"), P("row", "col"), P("row", "col"))
    out_specs = (P("row", "col"), P("row", "col"), P("row", "col"))
    return jax.shard_map(shards, mesh=mesh, in_specs=in_specs, out_specs=out_specs, check_vma=False)
```

```python
import functools

import jax
import jax.numpy as jnp
from jax import lax
from jax.experimental import pallas as pl
from jax.experimental.pallas import tpu as pltpu
from jax.sharding import PartitionSpec as P

BLOCK = 128
TILE = 8


def full_dot(left, right, dims):
    return lax.dot_general(
        left, right, (dims, ((), ())), precision=lax.Precision.HIGHEST, preferred_element_type=jnp.float32
    )


def one_hot_dot(value, move, pieces):
    total = None
    rest = value
    for _ in range(pieces):
        piece = rest.astype(jnp.bfloat16)
        rest = rest - piece.astype(jnp.float32)
        part = lax.dot_general(move, piece, (((1,), (0,)), ((), ())), preferred_element_type=jnp.float32)
        total = part if total is None else total + part
    return total


def eliminate(s_ref, r_ref, base):
    count = BLOCK // TILE
    shape = (TILE, BLOCK)
    lane = lax.broadcasted_iota(jnp.int32, shape, 1)
    tiles = [s_ref[pl.ds(base + t * TILE, TILE), pl.ds(base, BLOCK)] for t in range(count)]
    for p in range(count):
        first = p * TILE
        own = tiles[p]
        rows = [jnp.broadcast_to(own[j : j + 1, :], shape) for j in range(TILE)]
        a = [
            [jnp.broadcast_to(rows[i][:, first + j : first + j + 1], shape) for j in range(i + 1)]
            for i in range(TILE)
        ]
        cols = {
            t: [jnp.broadcast_to(tiles[t][:, first + j : first + j + 1], shape) for j in range(TILE)]
            for t in range(p + 1, count)
        }
        for k in range(TILE):
            scale = lax.rsqrt(a[k][k])
            low = [a[i][k] * scale for i in range(k + 1, TILE)]
            row = rows[k] * scale
            r_ref[first + k : first + k + 1, :] = row[0:1, :]
            used = row + jnp.where(lane == first + k, scale, 0.0)
            for i in range(k + 1, TILE):
                rows[i] = rows[i] - low[i - k - 1] * used
                for j in range(k + 1, i + 1):
                    a[i][j] = a[i][j] - low[i - k - 1] * low[j - k - 1]
            for t in range(p + 1, count):
                col = cols[t][k] * scale
                tiles[t] = tiles[t] - col * used
                for j in range(k + 1, TILE):
                    cols[t][j] = cols[t][j] - col * low[j - k - 1]


def split(value):
    high = value.astype(jnp.bfloat16)
    return high, (value - high.astype(jnp.float32)).astype(jnp.bfloat16)


def split_rows(value):
    high, low = split(value)
    return jnp.concatenate([high, high, low], axis=0)


def split_dot(left, right_parts):
    high, low = split(left)
    return lax.dot_general(
        jnp.concatenate([high, low, high], axis=1),
        right_parts,
        (((1,), (0,)), ((), ())),
        preferred_element_type=jnp.float32,
    )


def factor_block(s_ref, l_ref, x_ref, r_ref, base):
    width = s_ref.shape[0]
    here = pl.ds(base, BLOCK)
    up = lax.broadcasted_iota(jnp.int32, (BLOCK, BLOCK), 0)
    across = lax.broadcasted_iota(jnp.int32, (BLOCK, BLOCK), 1)
    row = lax.broadcasted_iota(jnp.int32, (width, BLOCK), 0)
    eliminate(s_ref, r_ref, base)
    both = r_ref[...]
    inv = jnp.where(up > across, both, 0.0) + jnp.where(up == across, 1.0 / both, 0.0)
    x_ref[here, :] = -full_dot(inv, full_dot(l_ref[here, :], x_ref[...], ((1,), (0,))), ((1,), (0,)))
    x_ref[here, here] = inv
    below = jnp.where(row >= base + BLOCK, full_dot(s_ref[:, here], inv, ((1,), (1,))), 0.0)
    l_ref[:, here] = below
    l_ref[here, here] = jnp.where(up >= across, both.T, 0.0)
    s_ref[...] = s_ref[...] - full_dot(below, below, ((1,), (1,)))


def finish_factor(row_count, col_count, f_ref, e_ref, q_ref, s_ref, l_ref, x_ref):
    width = s_ref.shape[0]
    r = lax.axis_index("row")
    c = lax.axis_index("col")
    per = width // col_count
    rows_dev = width // row_count
    i0 = lax.broadcasted_iota(jnp.int32, (rows_dev, width), 0)
    i1 = lax.broadcasted_iota(jnp.int32, (rows_dev, width), 1)
    pick_rows = jnp.where(i1 == i0 * row_count + r, 1.0, 0.0)
    j0 = lax.broadcasted_iota(jnp.int32, (per, width), 0)
    j1 = lax.broadcasted_iota(jnp.int32, (per, width), 1)
    pick_cols = jnp.where(j1 == j0 * col_count + c, 1.0, 0.0)
    f_ref[...] = full_dot(full_dot(pick_rows, l_ref[...], ((1,), (0,))), pick_cols, ((1,), (1,)))
    natural = lax.broadcasted_iota(jnp.int32, (width, width), 0)
    store = lax.broadcasted_iota(jnp.int32, (width, width), 1)
    from_cols = jnp.where(natural == (store % per) * col_count + store // per, 1.0, 0.0)
    s_ref[...] = full_dot(x_ref[...], from_cols, ((1,), (0,)))
    e_ref[...] = split_rows(full_dot(s_ref[...], pick_cols, ((0,), (1,))))
    q_ref[...] = split_rows(full_dot(s_ref[...], s_ref[...], ((0,), (0,))))


def to_natural(row_count, col_count, g_ref, s_ref, x_ref):
    width = s_ref.shape[0]
    per = width // col_count
    rows_dev = width // row_count
    for r in range(row_count):
        for z in range(col_count):
            s_ref[r * rows_dev : (r + 1) * rows_dev, z * per : (z + 1) * per] = g_ref[r, z]
    natural = lax.broadcasted_iota(jnp.int32, (width, width), 0)
    store = lax.broadcasted_iota(jnp.int32, (width, width), 1)
    from_rows = jnp.where(natural == (store % rows_dev) * row_count + store // rows_dev, 1.0, 0.0)
    from_cols = jnp.where(natural == (store % per) * col_count + store // per, 1.0, 0.0)
    x_ref[...] = one_hot_dot(s_ref[...], from_rows.astype(jnp.bfloat16), 3)
    s_ref[...] = one_hot_dot(x_ref[...].T, from_cols.astype(jnp.bfloat16), 3)


def top_solve(col_count, q_ref, top_ref, t_ref, o_ref):
    groups, length, _ = top_ref.shape
    owners = groups // col_count
    width = q_ref.shape[1]
    for h in range(owners):
        left = jnp.concatenate([top_ref[h * col_count + z] for z in range(col_count)], axis=1)
        solved = split_dot(left, q_ref[...])
        for b in range(width // BLOCK):
            t_ref[b, pl.ds(h, length, stride=owners), :] = solved[:, b * BLOCK : (b + 1) * BLOCK]
    for b in range(width // BLOCK):
        high, low = split(t_ref[b].T)
        at = b * BLOCK
        o_ref[at : at + BLOCK, :] = high
        o_ref[width + at : width + at + BLOCK, :] = high
        o_ref[2 * width + at : 2 * width + at + BLOCK, :] = low


def main_kernel(row_count, n, d_ref, p_ref, f_ref, e_ref, o_ref, buf_ref, *scratch):
    g_ref, top_ref, s_ref, l_ref, x_ref, r_ref, q_ref, t_ref = scratch[:8]
    own_sem, mine_send, mine_recv, col_send, col_recv, row_send, row_recv = scratch[8:15]
    piece_send, piece_recv, line_send, line_recv = scratch[15:]
    r = lax.axis_index("row")
    c = lax.axis_index("col")
    mesh_id = pl.DeviceIdType.MESH
    chunks = line_recv.shape[1]
    length = p_ref.shape[0] // chunks
    top_length = top_ref.shape[1]
    along_col = [(r, lax.rem(c + d, n)) for d in range(1, n)]
    along_row = [(lax.rem(r + d, row_count), c) for d in range(1, row_count)]
    q = lax.rem(r, n)
    swap_row = r - q + c
    barrier = pltpu.get_barrier_semaphore()
    for peer in along_col + along_row:
        pl.semaphore_signal(barrier, inc=1, device_id=peer, device_id_type=mesh_id)

    @pl.when(q != c)
    def _():
        pl.semaphore_signal(barrier, inc=1, device_id=(swap_row, q), device_id_type=mesh_id)
        pl.semaphore_wait(barrier, row_count + n - 1)

    @pl.when(q == c)
    def _():
        pl.semaphore_wait(barrier, row_count + n - 2)

    def remote(src, dst, send, recv, peer):
        return pltpu.make_async_remote_copy(
            src_ref=src, dst_ref=dst, send_sem=send, recv_sem=recv, device_id=peer, device_id_type=mesh_id
        )

    def line(phase, way, k):
        block = c - way * (phase - 1)
        part = pl.ds(pl.multiple_of(k * length, length), length)
        dst = buf_ref.at[block, part]
        src = p_ref.at[part] if phase == 1 else dst
        side = phase * 2 - 2 + (way + 1) // 2
        return remote(src, dst, line_send.at[side, k], line_recv.at[block, k], (r, c + way))

    def exists(phase, way):
        block = c - way * (phase - 1)
        return (block >= 0) & (block < n)

    def leaves(phase, way):
        return exists(phase, way) & (c + way >= 0) & (c + way < n)

    def forward(phase, k):
        for way in (1, -1):

            @pl.when(exists(phase, way))
            def _():
                line(phase, way, k).wait_recv()

            @pl.when(leaves(phase, way))
            def _():
                line(phase, way, k).start()

    own = pltpu.make_async_copy(d_ref, g_ref.at[r, c], own_sem)
    across = [
        remote(d_ref, g_ref.at[r, c], col_send.at[i], col_recv.at[i], peer) for i, peer in enumerate(along_col)
    ]
    for copy in [own] + across:
        copy.start()
    top = p_ref.at[pl.ds(0, top_length)]
    mine = remote(top, top_ref.at[swap_row], mine_send, mine_recv, (swap_row, q))
    keep = pltpu.make_async_copy(top, top_ref.at[r], mine_recv)

    @pl.when(q != c)
    def _():
        mine.start()

    @pl.when(q == c)
    def _():
        keep.start()

    def first(k, carry):
        for way in (1, -1):

            @pl.when(leaves(1, way))
            def _():
                line(1, way, k).start()

        return carry

    lax.fori_loop(0, chunks, first, 0)
    for copy in [own] + across:
        copy.wait()
    rows = [
        remote(g_ref.at[r], g_ref.at[r], row_send.at[i], row_recv.at[i], peer) for i, peer in enumerate(along_row)
    ]
    for copy in rows:
        copy.start()

    @pl.when(q != c)
    def _():
        mine.wait()

    @pl.when(q == c)
    def _():
        keep.wait()

    pieces = [
        remote(top_ref.at[r], top_ref.at[r], piece_send.at[i], piece_recv.at[i], peer)
        for i, peer in enumerate(along_row)
    ]
    for copy in pieces:
        copy.start()
    for copy in rows:
        copy.wait()
    to_natural(row_count, n, g_ref, s_ref, x_ref)
    l_ref[...] = jnp.zeros_like(l_ref)
    x_ref[...] = jnp.zeros_like(x_ref)

    def step(k, carry):
        factor_block(s_ref, l_ref, x_ref, r_ref, pl.multiple_of(k * BLOCK, BLOCK))
        forward(2, k)
        return carry

    lax.fori_loop(0, chunks, step, 0)
    finish_factor(row_count, n, f_ref, e_ref, q_ref, s_ref, l_ref, x_ref)
    for copy in pieces:
        copy.wait()
    top_solve(n, q_ref, top_ref, t_ref, o_ref)
    for phase in range(3, n + 1):

        def later(k, carry, phase=phase):
            forward(phase, k)
            return carry

        lax.fori_loop(0, chunks, later, 0)
    for phase in range(1, n):

        def drain(k, carry, phase=phase):
            for way in (1, -1):

                @pl.when(leaves(phase, way))
                def _():
                    line(phase, way, k).wait_send()

            return carry

        lax.fori_loop(0, chunks, drain, 0)


def exchange(block, panel, columns, row_count, n):
    dma = pltpu.SemaphoreType.DMA
    rows, lanes = panel.shape
    width = block.shape[0] * row_count
    chunks = width // BLOCK
    top_length = columns // (row_count // n)
    square = pltpu.VMEM((width, width), jnp.float32)
    return pl.pallas_call(
        functools.partial(main_kernel, row_count, n),
        out_shape=(
            jax.ShapeDtypeStruct(block.shape, jnp.float32),
            jax.ShapeDtypeStruct((3 * width, lanes), jnp.bfloat16),
            jax.ShapeDtypeStruct((3 * width, columns), jnp.bfloat16),
            jax.ShapeDtypeStruct((n, rows, lanes), jnp.float32),
        ),
        in_specs=[pl.BlockSpec(memory_space=pltpu.VMEM), pl.BlockSpec(memory_space=pl.ANY)],
        out_specs=(pl.BlockSpec(memory_space=pltpu.VMEM),) * 3 + (pl.BlockSpec(memory_space=pl.ANY),),
        scratch_shapes=[
            pltpu.VMEM((row_count, n) + block.shape, jnp.float32),
            pltpu.VMEM((row_count, top_length, lanes), jnp.float32),
            square, square, square,
            pltpu.VMEM((BLOCK, BLOCK), jnp.float32),
            pltpu.VMEM((3 * width, width), jnp.bfloat16),
            pltpu.VMEM((width // BLOCK, columns, BLOCK), jnp.float32),
            dma, dma, dma, dma((n - 1,)), dma((n - 1,)), dma((row_count - 1,)), dma((row_count - 1,)),
            dma((row_count - 1,)), dma((row_count - 1,)), dma((2 * n - 2, chunks)), dma((n, chunks)),
        ],
        compiler_params=pltpu.CompilerParams(
            collective_id=0, has_side_effects=True, vmem_limit_bytes=56 * 1024 * 1024
        ),
    )(block, panel)


def update_kernel(p_ref, b_ref, e_ref, t_ref, c_ref, f_ref, n_ref):
    count = b_ref.shape[0]
    c = lax.axis_index("col")
    own = p_ref[...]
    pieces = [jnp.where(c == z, own, b_ref[z]) for z in range(count)]
    high, low = split(jnp.concatenate(pieces, axis=1))
    left = jnp.concatenate([high, low, high], axis=1)
    dims = (((1,), (0,)), ((), ()))
    f_ref[...] = lax.dot_general(left, e_ref[...], dims, preferred_element_type=jnp.float32)
    n_ref[...] = c_ref[...] - lax.dot_general(left, t_ref[...], dims, preferred_element_type=jnp.float32)


def update_rows(panel, gathered, e_parts, top_parts, trailing):
    n, rows, lanes = gathered.shape
    columns = trailing.shape[1]
    tile = 256
    fixed = lambda a: pl.BlockSpec(a.shape, lambda i: (0, 0), pipeline_mode=pl.Buffered(1))
    strip = lambda w: pl.BlockSpec((tile, w), lambda i: (i, 0))
    flops = 2 * rows * top_parts.shape[0] * (columns + lanes)
    return pl.pallas_call(
        update_kernel,
        grid=(rows // tile,),
        out_shape=(
            jax.ShapeDtypeStruct((rows, lanes), jnp.float32),
            jax.ShapeDtypeStruct((rows, columns), jnp.float32),
        ),
        in_specs=[
            strip(lanes),
            pl.BlockSpec((n, tile, lanes), lambda i: (0, i, 0)),
            fixed(e_parts),
            fixed(top_parts),
            strip(columns),
        ],
        out_specs=(strip(lanes), strip(columns)),
        cost_estimate=pl.CostEstimate(flops=flops, bytes_accessed=rows * columns * 8, transcendentals=0),
        compiler_params=pltpu.CompilerParams(vmem_limit_bytes=60 * 1024 * 1024),
    )(panel, gathered, e_parts, top_parts, trailing)


def shards(diag_block, panel_below, trailing):
    row_count = lax.axis_size("row")
    n = lax.axis_size("col")
    diag_factor, e_parts, top_parts, gathered = exchange(diag_block, panel_below, trailing.shape[1], row_count, n)
    return (diag_factor, *update_rows(panel_below, gathered, e_parts, top_parts, trailing))


def solution(mesh):
    in_specs = (P("row", "col"), P("row", "col"), P("row", "col"))
    out_specs = (P("row", "col"), P("row", "col"), P("row", "col"))
    return jax.shard_map(shards, mesh=mesh, in_specs=in_specs, out_specs=out_specs, check_vma=False)
```

```python
import functools

import jax
import jax.numpy as jnp
from jax import lax
from jax.experimental import pallas as pl
from jax.experimental.pallas import tpu as pltpu
from jax.sharding import PartitionSpec as P

BLOCK = 128
TILE = 8


def full_dot(left, right, dims):
    return lax.dot_general(
        left, right, (dims, ((), ())), precision=lax.Precision.HIGHEST, preferred_element_type=jnp.float32
    )


def one_hot_dot(value, move, pieces):
    total = None
    rest = value
    for _ in range(pieces):
        piece = rest.astype(jnp.bfloat16)
        rest = rest - piece.astype(jnp.float32)
        part = lax.dot_general(move, piece, (((1,), (0,)), ((), ())), preferred_element_type=jnp.float32)
        total = part if total is None else total + part
    return total


def eliminate(s_ref, r_ref, base):
    count = BLOCK // TILE
    shape = (TILE, BLOCK)
    lane = lax.broadcasted_iota(jnp.int32, shape, 1)
    tiles = [s_ref[pl.ds(base + t * TILE, TILE), pl.ds(base, BLOCK)] for t in range(count)]
    for p in range(count):
        first = p * TILE
        own = tiles[p]
        rows = [jnp.broadcast_to(own[j : j + 1, :], shape) for j in range(TILE)]
        a = [
            [jnp.broadcast_to(rows[i][:, first + j : first + j + 1], shape) for j in range(i + 1)]
            for i in range(TILE)
        ]
        cols = {
            t: [jnp.broadcast_to(tiles[t][:, first + j : first + j + 1], shape) for j in range(TILE)]
            for t in range(p + 1, count)
        }
        for k in range(TILE):
            scale = lax.rsqrt(a[k][k])
            low = [a[i][k] * scale for i in range(k + 1, TILE)]
            row = rows[k] * scale
            r_ref[first + k : first + k + 1, :] = row[0:1, :]
            used = row + jnp.where(lane == first + k, scale, 0.0)
            for i in range(k + 1, TILE):
                rows[i] = rows[i] - low[i - k - 1] * used
                for j in range(k + 1, i + 1):
                    a[i][j] = a[i][j] - low[i - k - 1] * low[j - k - 1]
            for t in range(p + 1, count):
                col = cols[t][k] * scale
                tiles[t] = tiles[t] - col * used
                for j in range(k + 1, TILE):
                    cols[t][j] = cols[t][j] - col * low[j - k - 1]


def split(value):
    high = value.astype(jnp.bfloat16)
    return high, (value - high.astype(jnp.float32)).astype(jnp.bfloat16)


def split_rows(value):
    high, low = split(value)
    return jnp.concatenate([high, high, low], axis=0)


def split_dot(left, right_parts):
    high, low = split(left)
    return lax.dot_general(
        jnp.concatenate([high, low, high], axis=1),
        right_parts,
        (((1,), (0,)), ((), ())),
        preferred_element_type=jnp.float32,
    )


def factor_block(s_ref, l_ref, x_ref, r_ref, base):
    width = s_ref.shape[0]
    here = pl.ds(base, BLOCK)
    up = lax.broadcasted_iota(jnp.int32, (BLOCK, BLOCK), 0)
    across = lax.broadcasted_iota(jnp.int32, (BLOCK, BLOCK), 1)
    row = lax.broadcasted_iota(jnp.int32, (width, BLOCK), 0)
    eliminate(s_ref, r_ref, base)
    both = r_ref[...]
    inv = jnp.where(up > across, both, 0.0) + jnp.where(up == across, 1.0 / both, 0.0)
    x_ref[here, :] = -full_dot(inv, full_dot(l_ref[here, :], x_ref[...], ((1,), (0,))), ((1,), (0,)))
    x_ref[here, here] = inv
    below = jnp.where(row >= base + BLOCK, full_dot(s_ref[:, here], inv, ((1,), (1,))), 0.0)
    l_ref[:, here] = below
    l_ref[here, here] = jnp.where(up >= across, both.T, 0.0)
    s_ref[...] = s_ref[...] - full_dot(below, below, ((1,), (1,)))


def finish_factor(row_count, col_count, f_ref, e_ref, q_ref, s_ref, l_ref, x_ref):
    width = s_ref.shape[0]
    r = lax.axis_index("row")
    c = lax.axis_index("col")
    per = width // col_count
    rows_dev = width // row_count
    i0 = lax.broadcasted_iota(jnp.int32, (rows_dev, width), 0)
    i1 = lax.broadcasted_iota(jnp.int32, (rows_dev, width), 1)
    pick_rows = jnp.where(i1 == i0 * row_count + r, 1.0, 0.0)
    j0 = lax.broadcasted_iota(jnp.int32, (per, width), 0)
    j1 = lax.broadcasted_iota(jnp.int32, (per, width), 1)
    pick_cols = jnp.where(j1 == j0 * col_count + c, 1.0, 0.0)
    f_ref[...] = full_dot(full_dot(pick_rows, l_ref[...], ((1,), (0,))), pick_cols, ((1,), (1,)))
    natural = lax.broadcasted_iota(jnp.int32, (width, width), 0)
    store = lax.broadcasted_iota(jnp.int32, (width, width), 1)
    from_cols = jnp.where(natural == (store % per) * col_count + store // per, 1.0, 0.0)
    s_ref[...] = full_dot(x_ref[...], from_cols, ((1,), (0,)))
    e_ref[...] = split_rows(full_dot(s_ref[...], pick_cols, ((0,), (1,))))
    q_ref[...] = split_rows(full_dot(s_ref[...], s_ref[...], ((0,), (0,))))


def to_natural(row_count, col_count, g_ref, s_ref, x_ref):
    width = s_ref.shape[0]
    per = width // col_count
    rows_dev = width // row_count
    for r in range(row_count):
        for z in range(col_count):
            s_ref[r * rows_dev : (r + 1) * rows_dev, z * per : (z + 1) * per] = g_ref[r, z]
    natural = lax.broadcasted_iota(jnp.int32, (width, width), 0)
    store = lax.broadcasted_iota(jnp.int32, (width, width), 1)
    from_rows = jnp.where(natural == (store % rows_dev) * row_count + store // rows_dev, 1.0, 0.0)
    from_cols = jnp.where(natural == (store % per) * col_count + store // per, 1.0, 0.0)
    x_ref[...] = one_hot_dot(s_ref[...], from_rows.astype(jnp.bfloat16), 3)
    s_ref[...] = one_hot_dot(x_ref[...].T, from_cols.astype(jnp.bfloat16), 3)


def top_solve(col_count, q_ref, top_ref, t_ref, o_ref):
    groups, length, _ = top_ref.shape
    owners = groups // col_count
    width = q_ref.shape[1]
    for h in range(owners):
        left = jnp.concatenate([top_ref[h * col_count + z] for z in range(col_count)], axis=1)
        solved = split_dot(left, q_ref[...])
        for b in range(width // BLOCK):
            t_ref[b, pl.ds(h, length, stride=owners), :] = solved[:, b * BLOCK : (b + 1) * BLOCK]
    for b in range(width // BLOCK):
        high, low = split(t_ref[b].T)
        at = b * BLOCK
        o_ref[at : at + BLOCK, :] = high
        o_ref[width + at : width + at + BLOCK, :] = high
        o_ref[2 * width + at : 2 * width + at + BLOCK, :] = low


def main_kernel(row_count, n, d_ref, p_ref, f_ref, e_ref, o_ref, buf_ref, *scratch):
    g_ref, top_ref, s_ref, l_ref, x_ref, r_ref, q_ref, t_ref = scratch[:8]
    own_sem, mine_send, mine_recv, col_send, col_recv, row_send, row_recv = scratch[8:15]
    piece_send, piece_recv, line_send, line_recv, fill_sem = scratch[15:]
    r = lax.axis_index("row")
    c = lax.axis_index("col")
    mesh_id = pl.DeviceIdType.MESH
    chunks = line_recv.shape[1]
    length = p_ref.shape[0] // chunks
    top_length = top_ref.shape[1]
    along_col = [(r, lax.rem(c + d, n)) for d in range(1, n)]
    along_row = [(lax.rem(r + d, row_count), c) for d in range(1, row_count)]
    q = lax.rem(r, n)
    swap_row = r - q + c
    barrier = pltpu.get_barrier_semaphore()
    for peer in along_col + along_row:
        pl.semaphore_signal(barrier, inc=1, device_id=peer, device_id_type=mesh_id)

    @pl.when(q != c)
    def _():
        pl.semaphore_signal(barrier, inc=1, device_id=(swap_row, q), device_id_type=mesh_id)
        pl.semaphore_wait(barrier, row_count + n - 1)

    @pl.when(q == c)
    def _():
        pl.semaphore_wait(barrier, row_count + n - 2)

    def remote(src, dst, send, recv, peer):
        return pltpu.make_async_remote_copy(
            src_ref=src, dst_ref=dst, send_sem=send, recv_sem=recv, device_id=peer, device_id_type=mesh_id
        )

    def line(phase, way, k):
        block = c - way * (phase - 1)
        part = pl.ds(pl.multiple_of(k * length, length), length)
        dst = buf_ref.at[block, part]
        src = p_ref.at[part] if phase == 1 else dst
        side = phase * 2 - 2 + (way + 1) // 2
        return remote(src, dst, line_send.at[side, k], line_recv.at[block, k], (r, c + way))

    def spare(where, k):
        return ((where == 0) | (where == n - 1)) & (q == where) & (k * length + length <= top_length)

    def exists(phase, way, k):
        block = c - way * (phase - 1)
        there = (block >= 0) & (block < n)
        return there if phase == 1 else there & jnp.logical_not(spare(c, k))

    def leaves(phase, way, k):
        block = c - way * (phase - 1)
        there = (block >= 0) & (block < n) & (c + way >= 0) & (c + way < n)
        return there & jnp.logical_not(spare(c + way, k))

    def forward(phase, k):
        for way in (1, -1):

            @pl.when(exists(phase, way, k))
            def _():
                line(phase, way, k).wait_recv()

            @pl.when(leaves(phase, way, k))
            def _():
                line(phase, way, k).start()

    own = pltpu.make_async_copy(d_ref, g_ref.at[r, c], own_sem)
    across = [
        remote(d_ref, g_ref.at[r, c], col_send.at[i], col_recv.at[i], peer) for i, peer in enumerate(along_col)
    ]
    for copy in [own] + across:
        copy.start()
    top = p_ref.at[pl.ds(0, top_length)]
    mine = remote(top, top_ref.at[swap_row], mine_send, mine_recv, (swap_row, q))
    keep = pltpu.make_async_copy(top, top_ref.at[r], mine_recv)

    @pl.when(q != c)
    def _():
        mine.start()

    @pl.when(q == c)
    def _():
        keep.start()

    def first(k, carry):
        for way in (1, -1):

            @pl.when(leaves(1, way, k))
            def _():
                line(1, way, k).start()

        return carry

    lax.fori_loop(0, chunks, first, 0)
    for copy in [own] + across:
        copy.wait()
    rows = [
        remote(g_ref.at[r], g_ref.at[r], row_send.at[i], row_recv.at[i], peer) for i, peer in enumerate(along_row)
    ]
    for copy in rows:
        copy.start()

    @pl.when(q != c)
    def _():
        mine.wait()

    @pl.when(q == c)
    def _():
        keep.wait()

    pieces = [
        remote(top_ref.at[r], top_ref.at[r], piece_send.at[i], piece_recv.at[i], peer)
        for i, peer in enumerate(along_row)
    ]
    for copy in pieces:
        copy.start()
    for copy in rows:
        copy.wait()
    to_natural(row_count, n, g_ref, s_ref, x_ref)
    l_ref[...] = jnp.zeros_like(l_ref)
    x_ref[...] = jnp.zeros_like(x_ref)

    def step(k, carry):
        factor_block(s_ref, l_ref, x_ref, r_ref, pl.multiple_of(k * BLOCK, BLOCK))
        forward(2, k)
        return carry

    lax.fori_loop(0, chunks, step, 0)
    finish_factor(row_count, n, f_ref, e_ref, q_ref, s_ref, l_ref, x_ref)
    half = chunks // 2

    def soon(k, carry):
        forward(3, k)
        return carry

    lax.fori_loop(0, half, soon, 0)
    for copy in pieces:
        copy.wait()
    spared = top_length // length * length
    ends = (q == c) & ((c == 0) | (c == n - 1))
    fill = []
    if spared:
        fill = [
            pltpu.make_async_copy(
                top_ref.at[r - q + z, pl.ds(0, spared)], buf_ref.at[z, pl.ds(0, spared)], fill_sem.at[z]
            )
            for z in range(n)
        ]

    @pl.when(ends)
    def _():
        for copy in fill:
            copy.start()

    top_solve(n, q_ref, top_ref, t_ref, o_ref)
    for phase in range(3, n + 1):

        def later(k, carry, phase=phase):
            forward(phase, k)
            return carry

        lax.fori_loop(half if phase == 3 else 0, chunks, later, 0)

    @pl.when(ends)
    def _():
        for copy in fill:
            copy.wait()

    for phase in range(1, n):

        def drain(k, carry, phase=phase):
            for way in (1, -1):

                @pl.when(leaves(phase, way, k))
                def _():
                    line(phase, way, k).wait_send()

            return carry

        lax.fori_loop(0, chunks, drain, 0)


def exchange(block, panel, columns, row_count, n):
    dma = pltpu.SemaphoreType.DMA
    rows, lanes = panel.shape
    width = block.shape[0] * row_count
    chunks = width // BLOCK
    top_length = columns // (row_count // n)
    square = pltpu.VMEM((width, width), jnp.float32)
    return pl.pallas_call(
        functools.partial(main_kernel, row_count, n),
        out_shape=(
            jax.ShapeDtypeStruct(block.shape, jnp.float32),
            jax.ShapeDtypeStruct((3 * width, lanes), jnp.bfloat16),
            jax.ShapeDtypeStruct((3 * width, columns), jnp.bfloat16),
            jax.ShapeDtypeStruct((n, rows, lanes), jnp.float32),
        ),
        in_specs=[pl.BlockSpec(memory_space=pltpu.VMEM), pl.BlockSpec(memory_space=pl.ANY)],
        out_specs=(pl.BlockSpec(memory_space=pltpu.VMEM),) * 3 + (pl.BlockSpec(memory_space=pl.ANY),),
        scratch_shapes=[
            pltpu.VMEM((row_count, n) + block.shape, jnp.float32),
            pltpu.VMEM((row_count, top_length, lanes), jnp.float32),
            square, square, square,
            pltpu.VMEM((BLOCK, BLOCK), jnp.float32),
            pltpu.VMEM((3 * width, width), jnp.bfloat16),
            pltpu.VMEM((width // BLOCK, columns, BLOCK), jnp.float32),
            dma, dma, dma, dma((n - 1,)), dma((n - 1,)), dma((row_count - 1,)), dma((row_count - 1,)),
            dma((row_count - 1,)), dma((row_count - 1,)), dma((2 * n - 2, chunks)), dma((n, chunks)),
            dma((n,)),
        ],
        compiler_params=pltpu.CompilerParams(
            collective_id=0, has_side_effects=True, vmem_limit_bytes=56 * 1024 * 1024
        ),
    )(block, panel)


def update_kernel(p_ref, b_ref, e_ref, t_ref, c_ref, f_ref, n_ref):
    count = b_ref.shape[0]
    c = lax.axis_index("col")
    own = p_ref[...]
    pieces = [jnp.where(c == z, own, b_ref[z]) for z in range(count)]
    high, low = split(jnp.concatenate(pieces, axis=1))
    left = jnp.concatenate([high, low, high], axis=1)
    dims = (((1,), (0,)), ((), ()))
    f_ref[...] = lax.dot_general(left, e_ref[...], dims, preferred_element_type=jnp.float32)
    n_ref[...] = c_ref[...] - lax.dot_general(left, t_ref[...], dims, preferred_element_type=jnp.float32)


def update_rows(panel, gathered, e_parts, top_parts, trailing):
    n, rows, lanes = gathered.shape
    columns = trailing.shape[1]
    tile = 256
    fixed = lambda a: pl.BlockSpec(a.shape, lambda i: (0, 0), pipeline_mode=pl.Buffered(1))
    strip = lambda w: pl.BlockSpec((tile, w), lambda i: (i, 0))
    flops = 2 * rows * top_parts.shape[0] * (columns + lanes)
    return pl.pallas_call(
        update_kernel,
        grid=(rows // tile,),
        out_shape=(
            jax.ShapeDtypeStruct((rows, lanes), jnp.float32),
            jax.ShapeDtypeStruct((rows, columns), jnp.float32),
        ),
        in_specs=[
            strip(lanes),
            pl.BlockSpec((n, tile, lanes), lambda i: (0, i, 0)),
            fixed(e_parts),
            fixed(top_parts),
            strip(columns),
        ],
        out_specs=(strip(lanes), strip(columns)),
        cost_estimate=pl.CostEstimate(flops=flops, bytes_accessed=rows * columns * 8, transcendentals=0),
        compiler_params=pltpu.CompilerParams(vmem_limit_bytes=60 * 1024 * 1024),
    )(panel, gathered, e_parts, top_parts, trailing)


def shards(diag_block, panel_below, trailing):
    row_count = lax.axis_size("row")
    n = lax.axis_size("col")
    diag_factor, e_parts, top_parts, gathered = exchange(diag_block, panel_below, trailing.shape[1], row_count, n)
    return (diag_factor, *update_rows(panel_below, gathered, e_parts, top_parts, trailing))


def solution(mesh):
    in_specs = (P("row", "col"), P("row", "col"), P("row", "col"))
    out_specs = (P("row", "col"), P("row", "col"), P("row", "col"))
    return jax.shard_map(shards, mesh=mesh, in_specs=in_specs, out_specs=out_specs, check_vma=False)
```

```python
import functools

import jax
import jax.numpy as jnp
from jax import lax
from jax.experimental import pallas as pl
from jax.experimental.pallas import tpu as pltpu
from jax.sharding import PartitionSpec as P

BLOCK = 128
TILE = 8
STRIP = 256


def full_dot(left, right, dims):
    return lax.dot_general(
        left, right, (dims, ((), ())), precision=lax.Precision.HIGHEST, preferred_element_type=jnp.float32
    )


def one_hot_dot(value, move, pieces):
    total = None
    rest = value
    for _ in range(pieces):
        piece = rest.astype(jnp.bfloat16)
        rest = rest - piece.astype(jnp.float32)
        part = lax.dot_general(move, piece, (((1,), (0,)), ((), ())), preferred_element_type=jnp.float32)
        total = part if total is None else total + part
    return total


def eliminate(s_ref, r_ref, base):
    count = BLOCK // TILE
    shape = (TILE, BLOCK)
    lane = lax.broadcasted_iota(jnp.int32, shape, 1)
    tiles = [s_ref[pl.ds(base + t * TILE, TILE), pl.ds(base, BLOCK)] for t in range(count)]
    for p in range(count):
        first = p * TILE
        own = tiles[p]
        rows = [jnp.broadcast_to(own[j : j + 1, :], shape) for j in range(TILE)]
        a = [
            [jnp.broadcast_to(rows[i][:, first + j : first + j + 1], shape) for j in range(i + 1)]
            for i in range(TILE)
        ]
        cols = {
            t: [jnp.broadcast_to(tiles[t][:, first + j : first + j + 1], shape) for j in range(TILE)]
            for t in range(p + 1, count)
        }
        for k in range(TILE):
            scale = lax.rsqrt(a[k][k])
            low = [a[i][k] * scale for i in range(k + 1, TILE)]
            row = rows[k] * scale
            r_ref[first + k : first + k + 1, :] = row[0:1, :]
            used = row + jnp.where(lane == first + k, scale, 0.0)
            for i in range(k + 1, TILE):
                rows[i] = rows[i] - low[i - k - 1] * used
                for j in range(k + 1, i + 1):
                    a[i][j] = a[i][j] - low[i - k - 1] * low[j - k - 1]
            for t in range(p + 1, count):
                col = cols[t][k] * scale
                tiles[t] = tiles[t] - col * used
                for j in range(k + 1, TILE):
                    cols[t][j] = cols[t][j] - col * low[j - k - 1]


def split(value):
    high = value.astype(jnp.bfloat16)
    return high, (value - high.astype(jnp.float32)).astype(jnp.bfloat16)


def split_rows(value):
    high, low = split(value)
    return jnp.concatenate([high, high, low], axis=0)


def split_dot(left, right_parts):
    high, low = split(left)
    return lax.dot_general(
        jnp.concatenate([high, low, high], axis=1),
        right_parts,
        (((1,), (0,)), ((), ())),
        preferred_element_type=jnp.float32,
    )


def factor_block(s_ref, l_ref, x_ref, r_ref, base):
    width = s_ref.shape[0]
    here = pl.ds(base, BLOCK)
    up = lax.broadcasted_iota(jnp.int32, (BLOCK, BLOCK), 0)
    across = lax.broadcasted_iota(jnp.int32, (BLOCK, BLOCK), 1)
    row = lax.broadcasted_iota(jnp.int32, (width, BLOCK), 0)
    eliminate(s_ref, r_ref, base)
    both = r_ref[...]
    inv = jnp.where(up > across, both, 0.0) + jnp.where(up == across, 1.0 / both, 0.0)
    x_ref[here, :] = -full_dot(inv, full_dot(l_ref[here, :], x_ref[...], ((1,), (0,))), ((1,), (0,)))
    x_ref[here, here] = inv
    below = jnp.where(row >= base + BLOCK, full_dot(s_ref[:, here], inv, ((1,), (1,))), 0.0)
    l_ref[:, here] = below
    l_ref[here, here] = jnp.where(up >= across, both.T, 0.0)
    s_ref[...] = s_ref[...] - full_dot(below, below, ((1,), (1,)))


def finish_factor(row_count, col_count, f_ref, e_ref, q_ref, s_ref, l_ref, x_ref):
    width = s_ref.shape[0]
    r = lax.axis_index("row")
    c = lax.axis_index("col")
    per = width // col_count
    rows_dev = width // row_count
    i0 = lax.broadcasted_iota(jnp.int32, (rows_dev, width), 0)
    i1 = lax.broadcasted_iota(jnp.int32, (rows_dev, width), 1)
    pick_rows = jnp.where(i1 == i0 * row_count + r, 1.0, 0.0)
    j0 = lax.broadcasted_iota(jnp.int32, (per, width), 0)
    j1 = lax.broadcasted_iota(jnp.int32, (per, width), 1)
    pick_cols = jnp.where(j1 == j0 * col_count + c, 1.0, 0.0)
    f_ref[...] = full_dot(full_dot(pick_rows, l_ref[...], ((1,), (0,))), pick_cols, ((1,), (1,)))
    natural = lax.broadcasted_iota(jnp.int32, (width, width), 0)
    store = lax.broadcasted_iota(jnp.int32, (width, width), 1)
    from_cols = jnp.where(natural == (store % per) * col_count + store // per, 1.0, 0.0)
    s_ref[...] = full_dot(x_ref[...], from_cols, ((1,), (0,)))
    e_ref[...] = split_rows(full_dot(s_ref[...], pick_cols, ((0,), (1,))))
    q_ref[...] = split_rows(full_dot(s_ref[...], s_ref[...], ((0,), (0,))))


def to_natural(row_count, col_count, g_ref, s_ref, x_ref):
    width = s_ref.shape[0]
    per = width // col_count
    rows_dev = width // row_count
    for r in range(row_count):
        for z in range(col_count):
            s_ref[r * rows_dev : (r + 1) * rows_dev, z * per : (z + 1) * per] = g_ref[r, z]
    natural = lax.broadcasted_iota(jnp.int32, (width, width), 0)
    store = lax.broadcasted_iota(jnp.int32, (width, width), 1)
    from_rows = jnp.where(natural == (store % rows_dev) * row_count + store // rows_dev, 1.0, 0.0)
    from_cols = jnp.where(natural == (store % per) * col_count + store // per, 1.0, 0.0)
    x_ref[...] = one_hot_dot(s_ref[...], from_rows.astype(jnp.bfloat16), 3)
    s_ref[...] = one_hot_dot(x_ref[...].T, from_cols.astype(jnp.bfloat16), 3)


def top_solve(col_count, q_ref, top_ref, t_ref, o_ref):
    groups, length, _ = top_ref.shape
    owners = groups // col_count
    width = q_ref.shape[1]
    for h in range(owners):
        left = jnp.concatenate([top_ref[h * col_count + z] for z in range(col_count)], axis=1)
        solved = split_dot(left, q_ref[...])
        for b in range(width // BLOCK):
            t_ref[b, pl.ds(h, length, stride=owners), :] = solved[:, b * BLOCK : (b + 1) * BLOCK]
    for b in range(width // BLOCK):
        high, low = split(t_ref[b].T)
        at = b * BLOCK
        o_ref[at : at + BLOCK, :] = high
        o_ref[width + at : width + at + BLOCK, :] = high
        o_ref[2 * width + at : 2 * width + at + BLOCK, :] = low


def strip_update(piece_ref, e_ref, t_ref, c_ref, f_ref, at):
    rows = pl.ds(at, STRIP)
    left = jnp.concatenate([piece_ref[z, rows] for z in range(piece_ref.shape[0])], axis=1)
    high, low = split(left)
    left = jnp.concatenate([high, low, high], axis=1)
    dims = (((1,), (0,)), ((), ()))
    f_ref[rows, :] = lax.dot_general(left, e_ref[...], dims, preferred_element_type=jnp.float32)
    c_ref[rows, :] = c_ref[rows, :] - lax.dot_general(left, t_ref[...], dims, preferred_element_type=jnp.float32)


def fetch_pieces(p_ref, buf_ref, piece_ref, sems, part):
    c = lax.axis_index("col")
    for z in range(piece_ref.shape[0]):

        @pl.when(c == z)
        def _():
            pltpu.make_async_copy(p_ref.at[part], piece_ref.at[z], sems.at[z]).start()

        @pl.when(c != z)
        def _():
            pltpu.make_async_copy(buf_ref.at[z, part], piece_ref.at[z], sems.at[z]).start()


def await_pieces(p_ref, piece_ref, sems, part):
    for z in range(piece_ref.shape[0]):
        pltpu.make_async_copy(p_ref.at[part], piece_ref.at[z], sems.at[z]).wait()


def main_kernel(row_count, n, d_ref, p_ref, c_ref, f_ref, e_out, o_out, buf_ref, part_f, part_n, *scratch):
    e_ref, o_ref, trail_ref, piece_ref, solved_ref, trail_in, trail_out, solved_out, piece_sem, keep_sem = scratch[:10]
    scratch = scratch[10:]
    g_ref, top_ref, s_ref, l_ref, x_ref, r_ref, q_ref, t_ref = scratch[:8]
    own_sem, mine_send, mine_recv, col_send, col_recv, row_send, row_recv = scratch[8:15]
    piece_send, piece_recv, line_send, line_recv, fill_sem = scratch[15:]
    r = lax.axis_index("row")
    c = lax.axis_index("col")
    mesh_id = pl.DeviceIdType.MESH
    chunks = line_recv.shape[1]
    length = p_ref.shape[0] // chunks
    top_length = top_ref.shape[1]
    along_col = [(r, lax.rem(c + d, n)) for d in range(1, n)]
    along_row = [(lax.rem(r + d, row_count), c) for d in range(1, row_count)]
    q = lax.rem(r, n)
    swap_row = r - q + c
    barrier = pltpu.get_barrier_semaphore()
    for peer in along_col + along_row:
        pl.semaphore_signal(barrier, inc=1, device_id=peer, device_id_type=mesh_id)

    @pl.when(q != c)
    def _():
        pl.semaphore_signal(barrier, inc=1, device_id=(swap_row, q), device_id_type=mesh_id)
        pl.semaphore_wait(barrier, row_count + n - 1)

    @pl.when(q == c)
    def _():
        pl.semaphore_wait(barrier, row_count + n - 2)

    def remote(src, dst, send, recv, peer):
        return pltpu.make_async_remote_copy(
            src_ref=src, dst_ref=dst, send_sem=send, recv_sem=recv, device_id=peer, device_id_type=mesh_id
        )

    def line(phase, way, k):
        block = c - way * (phase - 1)
        part = pl.ds(pl.multiple_of(k * length, length), length)
        dst = buf_ref.at[block, part]
        src = p_ref.at[part] if phase == 1 else dst
        side = phase * 2 - 2 + (way + 1) // 2
        return remote(src, dst, line_send.at[side, k], line_recv.at[block, k], (r, c + way))

    def spare(where, k):
        return ((where == 0) | (where == n - 1)) & (q == where) & (k * length + length <= top_length)

    def exists(phase, way, k):
        block = c - way * (phase - 1)
        there = (block >= 0) & (block < n)
        return there if phase == 1 else there & jnp.logical_not(spare(c, k))

    def leaves(phase, way, k):
        block = c - way * (phase - 1)
        there = (block >= 0) & (block < n) & (c + way >= 0) & (c + way < n)
        return there & jnp.logical_not(spare(c + way, k))

    def forward(phase, k):
        for way in (1, -1):

            @pl.when(exists(phase, way, k))
            def _():
                line(phase, way, k).wait_recv()

            @pl.when(leaves(phase, way, k))
            def _():
                line(phase, way, k).start()

    own = pltpu.make_async_copy(d_ref, g_ref.at[r, c], own_sem)
    across = [
        remote(d_ref, g_ref.at[r, c], col_send.at[i], col_recv.at[i], peer) for i, peer in enumerate(along_col)
    ]
    for copy in [own] + across:
        copy.start()
    top = p_ref.at[pl.ds(0, top_length)]
    mine = remote(top, top_ref.at[swap_row], mine_send, mine_recv, (swap_row, q))
    keep = pltpu.make_async_copy(top, top_ref.at[r], mine_recv)

    @pl.when(q != c)
    def _():
        mine.start()

    @pl.when(q == c)
    def _():
        keep.start()

    def first(k, carry):
        for way in (1, -1):

            @pl.when(leaves(1, way, k))
            def _():
                line(1, way, k).start()

        return carry

    lax.fori_loop(0, chunks, first, 0)
    done = chunks - 1

    def span(k):
        return pl.ds(pl.multiple_of(k * length, length), length)

    def load(k):
        return pltpu.make_async_copy(c_ref.at[span(k)], trail_ref.at[k], trail_in.at[k])

    def save(k):
        return (
            pltpu.make_async_copy(trail_ref.at[k], part_n.at[span(k)], trail_out.at[k]),
            pltpu.make_async_copy(solved_ref.at[k], part_f.at[span(k)], solved_out.at[k]),
        )

    for copy in [own] + across:
        copy.wait()
    rows = [
        remote(g_ref.at[r], g_ref.at[r], row_send.at[i], row_recv.at[i], peer) for i, peer in enumerate(along_row)
    ]
    for copy in rows:
        copy.start()

    @pl.when(q != c)
    def _():
        mine.wait()

    @pl.when(q == c)
    def _():
        keep.wait()

    pieces = [
        remote(top_ref.at[r], top_ref.at[r], piece_send.at[i], piece_recv.at[i], peer)
        for i, peer in enumerate(along_row)
    ]
    for copy in pieces:
        copy.start()
    for copy in rows:
        copy.wait()
    for k in range(done):
        load(k).start()
    to_natural(row_count, n, g_ref, s_ref, x_ref)
    l_ref[...] = jnp.zeros_like(l_ref)
    x_ref[...] = jnp.zeros_like(x_ref)

    def step(k, carry):
        factor_block(s_ref, l_ref, x_ref, r_ref, pl.multiple_of(k * BLOCK, BLOCK))
        forward(2, k)
        return carry

    lax.fori_loop(0, chunks, step, 0)
    finish_factor(row_count, n, f_ref, e_ref, q_ref, s_ref, l_ref, x_ref)
    half = chunks // 2

    def soon(k, carry):
        forward(3, k)
        return carry

    lax.fori_loop(0, half, soon, 0)
    for copy in pieces:
        copy.wait()
    spared = top_length // length * length
    ends = (q == c) & ((c == 0) | (c == n - 1))
    fill = []
    if spared:
        fill = [
            pltpu.make_async_copy(
                top_ref.at[r - q + z, pl.ds(0, spared)], buf_ref.at[z, pl.ds(0, spared)], fill_sem.at[z]
            )
            for z in range(n)
        ]

    @pl.when(ends)
    def _():
        for copy in fill:
            copy.start()

    top_solve(n, q_ref, top_ref, t_ref, o_ref)
    keeps = [
        pltpu.make_async_copy(e_ref, e_out, keep_sem.at[0]),
        pltpu.make_async_copy(o_ref, o_out, keep_sem.at[1]),
    ]
    for copy in keeps:
        copy.start()
    for phase in range(3, n):

        def later(k, carry, phase=phase):
            forward(phase, k)
            return carry

        lax.fori_loop(half if phase == 3 else 0, chunks, later, 0)

    @pl.when(ends)
    def _():
        for copy in fill:
            copy.wait()

    def update(k, carry):
        forward(n, k)
        fetch_pieces(p_ref, buf_ref, piece_ref, piece_sem, span(k))
        load(k).wait()
        await_pieces(p_ref, piece_ref, piece_sem, span(k))

        def strip(i, carry):
            at = pl.multiple_of(i * STRIP, STRIP)
            strip_update(piece_ref, e_ref, o_ref, trail_ref.at[k], solved_ref.at[k], at)
            return carry

        lax.fori_loop(0, length // STRIP, strip, 0)
        for copy in save(k):
            copy.start()
        return carry

    lax.fori_loop(0, done, update, 0)
    forward(n, chunks - 1)
    for copy in keeps:
        copy.wait()
    for k in range(done):
        for copy in save(k):
            copy.wait()
    for phase in range(1, n):

        def drain(k, carry, phase=phase):
            for way in (1, -1):

                @pl.when(leaves(phase, way, k))
                def _():
                    line(phase, way, k).wait_send()

            return carry

        lax.fori_loop(0, chunks, drain, 0)


def exchange(block, panel, trailing, row_count, n):
    dma = pltpu.SemaphoreType.DMA
    rows, lanes = panel.shape
    columns = trailing.shape[1]
    width = block.shape[0] * row_count
    chunks = width // BLOCK
    length = rows // chunks
    done = chunks - 1
    top_length = columns // (row_count // n)
    square = pltpu.VMEM((width, width), jnp.float32)
    anywhere = pl.BlockSpec(memory_space=pl.ANY)
    vmem = pl.BlockSpec(memory_space=pltpu.VMEM)
    return pl.pallas_call(
        functools.partial(main_kernel, row_count, n),
        out_shape=(
            jax.ShapeDtypeStruct(block.shape, jnp.float32),
            jax.ShapeDtypeStruct((3 * width, lanes), jnp.bfloat16),
            jax.ShapeDtypeStruct((3 * width, columns), jnp.bfloat16),
            jax.ShapeDtypeStruct((n, rows, lanes), jnp.float32),
            jax.ShapeDtypeStruct((done * length, lanes), jnp.float32),
            jax.ShapeDtypeStruct((done * length, columns), jnp.float32),
        ),
        in_specs=[vmem, anywhere, anywhere],
        out_specs=(vmem,) + (anywhere,) * 5,
        scratch_shapes=[
            pltpu.VMEM((3 * width, lanes), jnp.bfloat16),
            pltpu.VMEM((3 * width, columns), jnp.bfloat16),
            pltpu.VMEM((done, length, columns), jnp.float32),
            pltpu.VMEM((n, length, lanes), jnp.float32),
            pltpu.VMEM((done, length, lanes), jnp.float32),
            dma((done,)), dma((done,)), dma((done,)), dma((n,)), dma((2,)),
            pltpu.VMEM((row_count, n) + block.shape, jnp.float32),
            pltpu.VMEM((row_count, top_length, lanes), jnp.float32),
            square, square, square,
            pltpu.VMEM((BLOCK, BLOCK), jnp.float32),
            pltpu.VMEM((3 * width, width), jnp.bfloat16),
            pltpu.VMEM((width // BLOCK, columns, BLOCK), jnp.float32),
            dma, dma, dma, dma((n - 1,)), dma((n - 1,)), dma((row_count - 1,)), dma((row_count - 1,)),
            dma((row_count - 1,)), dma((row_count - 1,)), dma((2 * n, chunks)), dma((n, chunks)),
            dma((n,)),
        ],
        compiler_params=pltpu.CompilerParams(
            collective_id=0, has_side_effects=True, vmem_limit_bytes=60 * 1024 * 1024
        ),
    )(block, panel, trailing)


def closing_kernel(p_ref, buf_ref, e_in, o_in, c_ref, part_f, part_n, f_ref, n_ref, *scratch):
    e_ref, o_ref, piece_ref, trail_ref, solved_ref, carry_f, carry_n = scratch[:7]
    keep_sem, piece_sem, trail_in, trail_out, solved_out, carry_in, carry_out = scratch[7:]
    strips = carry_n.shape[0]
    length = trail_ref.shape[0]
    start = p_ref.shape[0] - length
    mine = length // STRIP
    copy = pltpu.make_async_copy
    keeps = [copy(e_in, e_ref, keep_sem.at[0]), copy(o_in, o_ref, keep_sem.at[1])]
    whole = [copy(part_f, carry_f, keep_sem.at[2]), copy(carry_f, f_ref.at[pl.ds(0, start)], keep_sem.at[3])]

    def rows(i):
        return pl.ds(i * STRIP, STRIP)

    loads = [copy(c_ref.at[pl.ds(start + i * STRIP, STRIP)], trail_ref.at[rows(i)], trail_in.at[i]) for i in range(mine)]
    brings = [copy(part_n.at[rows(i)], carry_n.at[i], carry_in.at[i]) for i in range(strips)]
    takes = [copy(carry_n.at[i], n_ref.at[rows(i)], carry_out.at[i]) for i in range(strips)]
    stores = [copy(trail_ref.at[rows(i)], n_ref.at[pl.ds(start + i * STRIP, STRIP)], trail_out.at[i]) for i in range(mine)]
    solved = copy(solved_ref, f_ref.at[pl.ds(start, length)], solved_out)
    part = pl.ds(start, length)
    fetch_pieces(p_ref, buf_ref, piece_ref, piece_sem, part)
    for item in keeps + loads[:1] + brings + loads[1:] + whole[:1]:
        item.start()
    await_pieces(p_ref, piece_ref, piece_sem, part)
    for item in keeps:
        item.wait()
    sent = 0
    for i in range(mine):
        loads[i].wait()
        strip_update(piece_ref, e_ref, o_ref, trail_ref, solved_ref, i * STRIP)
        until = strips * (i + 1) // mine
        for j in range(sent, until):
            brings[j].wait()
            takes[j].start()
        sent = until
        stores[i].start()
    whole[0].wait()
    whole[1].start()
    solved.start()
    for item in takes + stores + [whole[1], solved]:
        item.wait()


def closing(panel, gathered, e_parts, top_parts, trailing, part_f, part_n):
    dma = pltpu.SemaphoreType.DMA
    n, rows, lanes = gathered.shape
    columns = trailing.shape[1]
    start = part_n.shape[0]
    length = rows - start
    anywhere = pl.BlockSpec(memory_space=pl.ANY)
    return pl.pallas_call(
        closing_kernel,
        out_shape=(
            jax.ShapeDtypeStruct((rows, lanes), jnp.float32),
            jax.ShapeDtypeStruct((rows, columns), jnp.float32),
        ),
        in_specs=[anywhere] * 7,
        out_specs=(anywhere,) * 2,
        scratch_shapes=[
            pltpu.VMEM(e_parts.shape, jnp.bfloat16),
            pltpu.VMEM(top_parts.shape, jnp.bfloat16),
            pltpu.VMEM((n, length, lanes), jnp.float32),
            pltpu.VMEM((length, columns), jnp.float32),
            pltpu.VMEM((length, lanes), jnp.float32),
            pltpu.VMEM((start, lanes), jnp.float32),
            pltpu.VMEM((start // STRIP, STRIP, columns), jnp.float32),
            dma((4,)), dma((n,)), dma((length // STRIP,)), dma((length // STRIP,)), dma,
            dma((start // STRIP,)), dma((start // STRIP,)),
        ],
        compiler_params=pltpu.CompilerParams(vmem_limit_bytes=60 * 1024 * 1024),
    )(panel, gathered, e_parts, top_parts, trailing, part_f, part_n)


def shards(diag_block, panel_below, trailing):
    row_count = lax.axis_size("row")
    n = lax.axis_size("col")
    diag_factor, *parts = exchange(diag_block, panel_below, trailing, row_count, n)
    gathered_parts = parts[2], parts[0], parts[1]
    return (diag_factor, *closing(panel_below, *gathered_parts, trailing, parts[3], parts[4]))


def solution(mesh):
    in_specs = (P("row", "col"), P("row", "col"), P("row", "col"))
    out_specs = (P("row", "col"), P("row", "col"), P("row", "col"))
    return jax.shard_map(shards, mesh=mesh, in_specs=in_specs, out_specs=out_specs, check_vma=False)
```

```python
import functools

import jax
import jax.numpy as jnp
from jax import lax
from jax.experimental import pallas as pl
from jax.experimental.pallas import tpu as pltpu
from jax.sharding import PartitionSpec as P

BLOCK = 128
TILE = 8
STRIP = 256


def full_dot(left, right, dims):
    return lax.dot_general(
        left, right, (dims, ((), ())), precision=lax.Precision.HIGHEST, preferred_element_type=jnp.float32
    )


def one_hot_dot(value, move, pieces):
    total = None
    rest = value
    for _ in range(pieces):
        piece = rest.astype(jnp.bfloat16)
        rest = rest - piece.astype(jnp.float32)
        part = lax.dot_general(move, piece, (((1,), (0,)), ((), ())), preferred_element_type=jnp.float32)
        total = part if total is None else total + part
    return total


def eliminate(s_ref, r_ref, base):
    count = BLOCK // TILE
    shape = (TILE, BLOCK)
    lane = lax.broadcasted_iota(jnp.int32, shape, 1)
    tiles = [s_ref[pl.ds(base + t * TILE, TILE), pl.ds(base, BLOCK)] for t in range(count)]
    for p in range(count):
        first = p * TILE
        own = tiles[p]
        rows = [jnp.broadcast_to(own[j : j + 1, :], shape) for j in range(TILE)]
        a = [
            [jnp.broadcast_to(rows[i][:, first + j : first + j + 1], shape) for j in range(i + 1)]
            for i in range(TILE)
        ]
        cols = {
            t: [jnp.broadcast_to(tiles[t][:, first + j : first + j + 1], shape) for j in range(TILE)]
            for t in range(p + 1, count)
        }
        for k in range(TILE):
            scale = lax.rsqrt(a[k][k])
            low = [a[i][k] * scale for i in range(k + 1, TILE)]
            row = rows[k] * scale
            r_ref[first + k : first + k + 1, :] = row[0:1, :]
            used = row + jnp.where(lane == first + k, scale, 0.0)
            for i in range(k + 1, TILE):
                rows[i] = rows[i] - low[i - k - 1] * used
                for j in range(k + 1, i + 1):
                    a[i][j] = a[i][j] - low[i - k - 1] * low[j - k - 1]
            for t in range(p + 1, count):
                col = cols[t][k] * scale
                tiles[t] = tiles[t] - col * used
                for j in range(k + 1, TILE):
                    cols[t][j] = cols[t][j] - col * low[j - k - 1]


def split(value):
    high = value.astype(jnp.bfloat16)
    return high, (value - high.astype(jnp.float32)).astype(jnp.bfloat16)


def split_rows(value):
    high, low = split(value)
    return jnp.concatenate([high, high, low], axis=0)


def split_dot(left, right_parts):
    high, low = split(left)
    return lax.dot_general(
        jnp.concatenate([high, low, high], axis=1),
        right_parts,
        (((1,), (0,)), ((), ())),
        preferred_element_type=jnp.float32,
    )


def factor_block(s_ref, l_ref, x_ref, r_ref, base):
    width = s_ref.shape[0]
    here = pl.ds(base, BLOCK)
    up = lax.broadcasted_iota(jnp.int32, (BLOCK, BLOCK), 0)
    across = lax.broadcasted_iota(jnp.int32, (BLOCK, BLOCK), 1)
    row = lax.broadcasted_iota(jnp.int32, (width, BLOCK), 0)
    eliminate(s_ref, r_ref, base)
    both = r_ref[...]
    inv = jnp.where(up > across, both, 0.0) + jnp.where(up == across, 1.0 / both, 0.0)
    x_ref[here, :] = -full_dot(inv, full_dot(l_ref[here, :], x_ref[...], ((1,), (0,))), ((1,), (0,)))
    x_ref[here, here] = inv
    below = jnp.where(row >= base + BLOCK, full_dot(s_ref[:, here], inv, ((1,), (1,))), 0.0)
    l_ref[:, here] = below
    l_ref[here, here] = jnp.where(up >= across, both.T, 0.0)
    s_ref[...] = s_ref[...] - full_dot(below, below, ((1,), (1,)))


def finish_factor(row_count, col_count, f_ref, e_ref, q_ref, s_ref, l_ref, x_ref):
    width = s_ref.shape[0]
    r = lax.axis_index("row")
    c = lax.axis_index("col")
    per = width // col_count
    rows_dev = width // row_count
    i0 = lax.broadcasted_iota(jnp.int32, (rows_dev, width), 0)
    i1 = lax.broadcasted_iota(jnp.int32, (rows_dev, width), 1)
    pick_rows = jnp.where(i1 == i0 * row_count + r, 1.0, 0.0)
    j0 = lax.broadcasted_iota(jnp.int32, (per, width), 0)
    j1 = lax.broadcasted_iota(jnp.int32, (per, width), 1)
    pick_cols = jnp.where(j1 == j0 * col_count + c, 1.0, 0.0)
    f_ref[...] = full_dot(full_dot(pick_rows, l_ref[...], ((1,), (0,))), pick_cols, ((1,), (1,)))
    natural = lax.broadcasted_iota(jnp.int32, (width, width), 0)
    store = lax.broadcasted_iota(jnp.int32, (width, width), 1)
    from_cols = jnp.where(natural == (store % per) * col_count + store // per, 1.0, 0.0)
    s_ref[...] = full_dot(x_ref[...], from_cols, ((1,), (0,)))
    e_ref[...] = split_rows(full_dot(s_ref[...], pick_cols, ((0,), (1,))))
    q_ref[...] = split_rows(full_dot(s_ref[...], s_ref[...], ((0,), (0,))))


def to_natural(row_count, col_count, g_ref, s_ref, x_ref):
    width = s_ref.shape[0]
    per = width // col_count
    rows_dev = width // row_count
    for r in range(row_count):
        for z in range(col_count):
            s_ref[r * rows_dev : (r + 1) * rows_dev, z * per : (z + 1) * per] = g_ref[r, z]
    natural = lax.broadcasted_iota(jnp.int32, (width, width), 0)
    store = lax.broadcasted_iota(jnp.int32, (width, width), 1)
    from_rows = jnp.where(natural == (store % rows_dev) * row_count + store // rows_dev, 1.0, 0.0)
    from_cols = jnp.where(natural == (store % per) * col_count + store // per, 1.0, 0.0)
    x_ref[...] = one_hot_dot(s_ref[...], from_rows.astype(jnp.bfloat16), 3)
    s_ref[...] = one_hot_dot(x_ref[...].T, from_cols.astype(jnp.bfloat16), 3)


def top_solve(col_count, q_ref, top_ref, t_ref, o_ref):
    groups, length, _ = top_ref.shape
    owners = groups // col_count
    width = q_ref.shape[1]
    for h in range(owners):
        left = jnp.concatenate([top_ref[h * col_count + z] for z in range(col_count)], axis=1)
        solved = split_dot(left, q_ref[...])
        for b in range(width // BLOCK):
            t_ref[b, pl.ds(h, length, stride=owners), :] = solved[:, b * BLOCK : (b + 1) * BLOCK]
    for b in range(width // BLOCK):
        high, low = split(t_ref[b].T)
        at = b * BLOCK
        o_ref[at : at + BLOCK, :] = high
        o_ref[width + at : width + at + BLOCK, :] = high
        o_ref[2 * width + at : 2 * width + at + BLOCK, :] = low


def strip_update(piece_ref, e_ref, t_ref, c_ref, f_ref, at):
    rows = pl.ds(at, STRIP)
    left = jnp.concatenate([piece_ref[z, rows] for z in range(piece_ref.shape[0])], axis=1)
    high, low = split(left)
    left = jnp.concatenate([high, low, high], axis=1)
    dims = (((1,), (0,)), ((), ()))
    f_ref[rows, :] = lax.dot_general(left, e_ref[...], dims, preferred_element_type=jnp.float32)
    c_ref[rows, :] = c_ref[rows, :] - lax.dot_general(left, t_ref[...], dims, preferred_element_type=jnp.float32)


def fetch_pieces(p_ref, buf_ref, piece_ref, sems, part):
    c = lax.axis_index("col")
    for z in range(piece_ref.shape[0]):

        @pl.when(c == z)
        def _():
            pltpu.make_async_copy(p_ref.at[part], piece_ref.at[z], sems.at[z]).start()

        @pl.when(c != z)
        def _():
            pltpu.make_async_copy(buf_ref.at[z, part], piece_ref.at[z], sems.at[z]).start()


def await_pieces(p_ref, piece_ref, sems, part):
    for z in range(piece_ref.shape[0]):
        pltpu.make_async_copy(p_ref.at[part], piece_ref.at[z], sems.at[z]).wait()


def main_kernel(row_count, n, d_ref, p_ref, c_ref, f_ref, e_out, o_out, buf_ref, part_f, part_n, *scratch):
    e_ref, o_ref, trail_ref, piece_ref, solved_ref, trail_in, trail_out, solved_out, piece_sem, keep_sem = scratch[:10]
    scratch = scratch[10:]
    g_ref, top_ref, s_ref, l_ref, x_ref, r_ref, q_ref, t_ref = scratch[:8]
    own_sem, mine_send, mine_recv, col_send, col_recv, row_send, row_recv = scratch[8:15]
    piece_send, piece_recv, line_send, line_recv, fill_sem = scratch[15:]
    r = lax.axis_index("row")
    c = lax.axis_index("col")
    mesh_id = pl.DeviceIdType.MESH
    chunks = line_recv.shape[1]
    length = p_ref.shape[0] // chunks
    top_length = top_ref.shape[1]
    along_col = [(r, lax.rem(c + d, n)) for d in range(1, n)]
    along_row = [(lax.rem(r + d, row_count), c) for d in range(1, row_count)]
    q = lax.rem(r, n)
    swap_row = r - q + c
    barrier = pltpu.get_barrier_semaphore()
    for peer in along_col + along_row:
        pl.semaphore_signal(barrier, inc=1, device_id=peer, device_id_type=mesh_id)

    @pl.when(q != c)
    def _():
        pl.semaphore_signal(barrier, inc=1, device_id=(swap_row, q), device_id_type=mesh_id)
        pl.semaphore_wait(barrier, row_count + n - 1)

    @pl.when(q == c)
    def _():
        pl.semaphore_wait(barrier, row_count + n - 2)

    def remote(src, dst, send, recv, peer):
        return pltpu.make_async_remote_copy(
            src_ref=src, dst_ref=dst, send_sem=send, recv_sem=recv, device_id=peer, device_id_type=mesh_id
        )

    def line(phase, way, k):
        block = c - way * (phase - 1)
        part = pl.ds(pl.multiple_of(k * length, length), length)
        dst = buf_ref.at[block, part]
        src = p_ref.at[part] if phase == 1 else dst
        side = phase * 2 - 2 + (way + 1) // 2
        return remote(src, dst, line_send.at[side, k], line_recv.at[block, k], (r, c + way))

    def spare(where, k):
        return ((where == 0) | (where == n - 1)) & (q == where) & (k * length + length <= top_length)

    def exists(phase, way, k):
        block = c - way * (phase - 1)
        there = (block >= 0) & (block < n)
        return there if phase == 1 else there & jnp.logical_not(spare(c, k))

    def leaves(phase, way, k):
        block = c - way * (phase - 1)
        there = (block >= 0) & (block < n) & (c + way >= 0) & (c + way < n)
        return there & jnp.logical_not(spare(c + way, k))

    def forward(phase, k):
        for way in (1, -1):

            @pl.when(exists(phase, way, k))
            def _():
                line(phase, way, k).wait_recv()

            @pl.when(leaves(phase, way, k))
            def _():
                line(phase, way, k).start()

    own = pltpu.make_async_copy(d_ref, g_ref.at[r, c], own_sem)
    across = [
        remote(d_ref, g_ref.at[r, c], col_send.at[i], col_recv.at[i], peer) for i, peer in enumerate(along_col)
    ]
    for copy in [own] + across:
        copy.start()
    top = p_ref.at[pl.ds(0, top_length)]
    mine = remote(top, top_ref.at[swap_row], mine_send, mine_recv, (swap_row, q))
    keep = pltpu.make_async_copy(top, top_ref.at[r], mine_recv)

    @pl.when(q != c)
    def _():
        mine.start()

    @pl.when(q == c)
    def _():
        keep.start()

    def first(k, carry):
        for way in (1, -1):

            @pl.when(leaves(1, way, k))
            def _():
                line(1, way, k).start()

        return carry

    lax.fori_loop(0, chunks, first, 0)
    done = chunks - 1

    def span(k):
        return pl.ds(pl.multiple_of(k * length, length), length)

    def load(k):
        return pltpu.make_async_copy(c_ref.at[span(k)], trail_ref.at[k], trail_in.at[k])

    def save(k):
        return (
            pltpu.make_async_copy(trail_ref.at[k], part_n.at[span(k)], trail_out.at[k]),
            pltpu.make_async_copy(solved_ref.at[k], part_f.at[span(k)], solved_out.at[k]),
        )

    for copy in [own] + across:
        copy.wait()
    rows = [
        remote(g_ref.at[r], g_ref.at[r], row_send.at[i], row_recv.at[i], peer) for i, peer in enumerate(along_row)
    ]
    for copy in rows:
        copy.start()

    pieces = [
        remote(top_ref.at[r], top_ref.at[r], piece_send.at[i], piece_recv.at[i], peer)
        for i, peer in enumerate(along_row)
    ]
    for copy in rows:
        copy.wait()
    for k in range(done):
        load(k).start()
    to_natural(row_count, n, g_ref, s_ref, x_ref)
    l_ref[...] = jnp.zeros_like(l_ref)
    x_ref[...] = jnp.zeros_like(x_ref)

    def step(k, carry):
        factor_block(s_ref, l_ref, x_ref, r_ref, pl.multiple_of(k * BLOCK, BLOCK))

        @pl.when(k == 0)
        def _():
            @pl.when(q != c)
            def _():
                mine.wait()

            @pl.when(q == c)
            def _():
                keep.wait()

            for copy in pieces:
                copy.start()
            forward(2, k)

        @pl.when(k < done)
        def _():
            forward(2, k + 1)

        @pl.when(k == done)
        def _():
            forward(3, k - done)

        return carry

    lax.fori_loop(0, chunks, step, 0)
    finish_factor(row_count, n, f_ref, e_ref, q_ref, s_ref, l_ref, x_ref)
    half = chunks // 2

    def soon(k, carry):
        forward(3, k)
        return carry

    lax.fori_loop(1, half, soon, 0)
    for copy in pieces:
        copy.wait()
    spared = top_length // length * length
    ends = (q == c) & ((c == 0) | (c == n - 1))
    fill = []
    if spared:
        fill = [
            pltpu.make_async_copy(
                top_ref.at[r - q + z, pl.ds(0, spared)], buf_ref.at[z, pl.ds(0, spared)], fill_sem.at[z]
            )
            for z in range(n)
        ]

    @pl.when(ends)
    def _():
        for copy in fill:
            copy.start()

    top_solve(n, q_ref, top_ref, t_ref, o_ref)
    keeps = [
        pltpu.make_async_copy(e_ref, e_out, keep_sem.at[0]),
        pltpu.make_async_copy(o_ref, o_out, keep_sem.at[1]),
    ]
    for copy in keeps:
        copy.start()
    for phase in range(3, n):

        def later(k, carry, phase=phase):
            forward(phase, k)
            return carry

        lax.fori_loop(half if phase == 3 else 0, chunks, later, 0)

    @pl.when(ends)
    def _():
        for copy in fill:
            copy.wait()

    def update(k, carry):
        forward(n, k)
        fetch_pieces(p_ref, buf_ref, piece_ref, piece_sem, span(k))
        load(k).wait()
        await_pieces(p_ref, piece_ref, piece_sem, span(k))

        def strip(i, carry):
            at = pl.multiple_of(i * STRIP, STRIP)
            strip_update(piece_ref, e_ref, o_ref, trail_ref.at[k], solved_ref.at[k], at)
            return carry

        lax.fori_loop(0, length // STRIP, strip, 0)
        for copy in save(k):
            copy.start()
        return carry

    lax.fori_loop(0, done, update, 0)
    forward(n, chunks - 1)
    for copy in keeps:
        copy.wait()
    for k in range(done):
        for copy in save(k):
            copy.wait()
    for phase in range(1, n):

        def drain(k, carry, phase=phase):
            for way in (1, -1):

                @pl.when(leaves(phase, way, k))
                def _():
                    line(phase, way, k).wait_send()

            return carry

        lax.fori_loop(0, chunks, drain, 0)


def exchange(block, panel, trailing, row_count, n):
    dma = pltpu.SemaphoreType.DMA
    rows, lanes = panel.shape
    columns = trailing.shape[1]
    width = block.shape[0] * row_count
    chunks = width // BLOCK
    length = rows // chunks
    done = chunks - 1
    top_length = columns // (row_count // n)
    square = pltpu.VMEM((width, width), jnp.float32)
    anywhere = pl.BlockSpec(memory_space=pl.ANY)
    vmem = pl.BlockSpec(memory_space=pltpu.VMEM)
    return pl.pallas_call(
        functools.partial(main_kernel, row_count, n),
        out_shape=(
            jax.ShapeDtypeStruct(block.shape, jnp.float32),
            jax.ShapeDtypeStruct((3 * width, lanes), jnp.bfloat16),
            jax.ShapeDtypeStruct((3 * width, columns), jnp.bfloat16),
            jax.ShapeDtypeStruct((n, rows, lanes), jnp.float32),
            jax.ShapeDtypeStruct((done * length, lanes), jnp.float32),
            jax.ShapeDtypeStruct((done * length, columns), jnp.float32),
        ),
        in_specs=[vmem, anywhere, anywhere],
        out_specs=(vmem,) + (anywhere,) * 5,
        scratch_shapes=[
            pltpu.VMEM((3 * width, lanes), jnp.bfloat16),
            pltpu.VMEM((3 * width, columns), jnp.bfloat16),
            pltpu.VMEM((done, length, columns), jnp.float32),
            pltpu.VMEM((n, length, lanes), jnp.float32),
            pltpu.VMEM((done, length, lanes), jnp.float32),
            dma((done,)), dma((done,)), dma((done,)), dma((n,)), dma((2,)),
            pltpu.VMEM((row_count, n) + block.shape, jnp.float32),
            pltpu.VMEM((row_count, top_length, lanes), jnp.float32),
            square, square, square,
            pltpu.VMEM((BLOCK, BLOCK), jnp.float32),
            pltpu.VMEM((3 * width, width), jnp.bfloat16),
            pltpu.VMEM((width // BLOCK, columns, BLOCK), jnp.float32),
            dma, dma, dma, dma((n - 1,)), dma((n - 1,)), dma((row_count - 1,)), dma((row_count - 1,)),
            dma((row_count - 1,)), dma((row_count - 1,)), dma((2 * n, chunks)), dma((n, chunks)),
            dma((n,)),
        ],
        compiler_params=pltpu.CompilerParams(
            collective_id=0, has_side_effects=True, vmem_limit_bytes=60 * 1024 * 1024
        ),
    )(block, panel, trailing)


def closing_kernel(p_ref, buf_ref, e_in, o_in, c_ref, part_f, part_n, d_in, d_out, f_ref, n_ref, *scratch):
    d_ref, e_ref, o_ref, piece_ref, trail_ref, solved_ref, carry_f, carry_n = scratch[:8]
    keep_sem, piece_sem, trail_in, trail_out, solved_out, carry_in, carry_out = scratch[8:]
    strips = carry_n.shape[0]
    length = trail_ref.shape[0]
    start = p_ref.shape[0] - length
    mine = length // STRIP
    copy = pltpu.make_async_copy
    keeps = [copy(e_in, e_ref, keep_sem.at[0]), copy(o_in, o_ref, keep_sem.at[1])]
    whole = [copy(part_f, carry_f, keep_sem.at[2]), copy(carry_f, f_ref.at[pl.ds(0, start)], keep_sem.at[3])]

    factor = [copy(d_in, d_ref, keep_sem.at[4]), copy(d_ref, d_out, keep_sem.at[5])]

    def rows(i):
        return pl.ds(i * STRIP, STRIP)

    loads = [copy(c_ref.at[pl.ds(start + i * STRIP, STRIP)], trail_ref.at[rows(i)], trail_in.at[i]) for i in range(mine)]
    brings = [copy(part_n.at[rows(i)], carry_n.at[i], carry_in.at[i]) for i in range(strips)]
    takes = [copy(carry_n.at[i], n_ref.at[rows(i)], carry_out.at[i]) for i in range(strips)]
    stores = [copy(trail_ref.at[rows(i)], n_ref.at[pl.ds(start + i * STRIP, STRIP)], trail_out.at[i]) for i in range(mine)]
    solved = copy(solved_ref, f_ref.at[pl.ds(start, length)], solved_out)
    part = pl.ds(start, length)
    fetch_pieces(p_ref, buf_ref, piece_ref, piece_sem, part)
    for item in keeps + loads[:1] + brings + loads[1:] + whole[:1] + factor[:1]:
        item.start()
    await_pieces(p_ref, piece_ref, piece_sem, part)
    for item in keeps:
        item.wait()
    sent = 0
    for i in range(mine):
        loads[i].wait()
        strip_update(piece_ref, e_ref, o_ref, trail_ref, solved_ref, i * STRIP)
        until = strips * (i + 1) // mine
        for j in range(sent, until):
            brings[j].wait()
            takes[j].start()
        sent = until
        stores[i].start()
    whole[0].wait()
    whole[1].start()
    factor[0].wait()
    factor[1].start()
    solved.start()
    for item in takes + stores + [whole[1], factor[1], solved]:
        item.wait()


def closing(panel, gathered, e_parts, top_parts, trailing, part_f, part_n, factor):
    dma = pltpu.SemaphoreType.DMA
    n, rows, lanes = gathered.shape
    columns = trailing.shape[1]
    start = part_n.shape[0]
    length = rows - start
    anywhere = pl.BlockSpec(memory_space=pl.ANY)
    return pl.pallas_call(
        closing_kernel,
        out_shape=(
            jax.ShapeDtypeStruct(factor.shape, jnp.float32),
            jax.ShapeDtypeStruct((rows, lanes), jnp.float32),
            jax.ShapeDtypeStruct((rows, columns), jnp.float32),
        ),
        in_specs=[anywhere] * 8,
        out_specs=(anywhere,) * 3,
        scratch_shapes=[
            pltpu.VMEM(factor.shape, jnp.float32),
            pltpu.VMEM(e_parts.shape, jnp.bfloat16),
            pltpu.VMEM(top_parts.shape, jnp.bfloat16),
            pltpu.VMEM((n, length, lanes), jnp.float32),
            pltpu.VMEM((length, columns), jnp.float32),
            pltpu.VMEM((length, lanes), jnp.float32),
            pltpu.VMEM((start, lanes), jnp.float32),
            pltpu.VMEM((start // STRIP, STRIP, columns), jnp.float32),
            dma((6,)), dma((n,)), dma((length // STRIP,)), dma((length // STRIP,)), dma,
            dma((start // STRIP,)), dma((start // STRIP,)),
        ],
        compiler_params=pltpu.CompilerParams(vmem_limit_bytes=60 * 1024 * 1024),
    )(panel, gathered, e_parts, top_parts, trailing, part_f, part_n, factor)


def shards(diag_block, panel_below, trailing):
    row_count = lax.axis_size("row")
    n = lax.axis_size("col")
    factor, e_parts, top_parts, gathered, part_f, part_n = exchange(diag_block, panel_below, trailing, row_count, n)
    return tuple(closing(panel_below, gathered, e_parts, top_parts, trailing, part_f, part_n, factor))


def solution(mesh):
    in_specs = (P("row", "col"), P("row", "col"), P("row", "col"))
    out_specs = (P("row", "col"), P("row", "col"), P("row", "col"))
    return jax.shard_map(shards, mesh=mesh, in_specs=in_specs, out_specs=out_specs, check_vma=False)
```

```python
import functools

import jax
import jax.numpy as jnp
from jax import lax
from jax.experimental import pallas as pl
from jax.experimental.pallas import tpu as pltpu
from jax.sharding import PartitionSpec as P

BLOCK = 128
TILE = 8
STRIP = 256


def full_dot(left, right, dims):
    return lax.dot_general(
        left, right, (dims, ((), ())), precision=lax.Precision.HIGHEST, preferred_element_type=jnp.float32
    )


def one_hot_dot(value, move, pieces):
    total = None
    rest = value
    for _ in range(pieces):
        piece = rest.astype(jnp.bfloat16)
        rest = rest - piece.astype(jnp.float32)
        part = lax.dot_general(move, piece, (((1,), (0,)), ((), ())), preferred_element_type=jnp.float32)
        total = part if total is None else total + part
    return total


def eliminate(s_ref, r_ref, base):
    count = BLOCK // TILE
    shape = (TILE, BLOCK)
    lane = lax.broadcasted_iota(jnp.int32, shape, 1)
    tiles = [s_ref[pl.ds(base + t * TILE, TILE), pl.ds(base, BLOCK)] for t in range(count)]
    for p in range(count):
        first = p * TILE
        own = tiles[p]
        rows = [jnp.broadcast_to(own[j : j + 1, :], shape) for j in range(TILE)]
        a = [
            [jnp.broadcast_to(rows[i][:, first + j : first + j + 1], shape) for j in range(i + 1)]
            for i in range(TILE)
        ]
        cols = {
            t: [jnp.broadcast_to(tiles[t][:, first + j : first + j + 1], shape) for j in range(TILE)]
            for t in range(p + 1, count)
        }
        for k in range(TILE):
            scale = lax.rsqrt(a[k][k])
            low = [a[i][k] * scale for i in range(k + 1, TILE)]
            row = rows[k] * scale
            r_ref[first + k : first + k + 1, :] = row[0:1, :]
            used = row + jnp.where(lane == first + k, scale, 0.0)
            for i in range(k + 1, TILE):
                rows[i] = rows[i] - low[i - k - 1] * used
                for j in range(k + 1, i + 1):
                    a[i][j] = a[i][j] - low[i - k - 1] * low[j - k - 1]
            for t in range(p + 1, count):
                col = cols[t][k] * scale
                tiles[t] = tiles[t] - col * used
                for j in range(k + 1, TILE):
                    cols[t][j] = cols[t][j] - col * low[j - k - 1]


def split(value):
    high = value.astype(jnp.bfloat16)
    return high, (value - high.astype(jnp.float32)).astype(jnp.bfloat16)


def split_rows(value):
    high, low = split(value)
    return jnp.concatenate([high, high, low], axis=0)


def split_dot(left, right_parts):
    high, low = split(left)
    return lax.dot_general(
        jnp.concatenate([high, low, high], axis=1),
        right_parts,
        (((1,), (0,)), ((), ())),
        preferred_element_type=jnp.float32,
    )


def factor_block(s_ref, l_ref, x_ref, r_ref, base):
    width = s_ref.shape[0]
    here = pl.ds(base, BLOCK)
    up = lax.broadcasted_iota(jnp.int32, (BLOCK, BLOCK), 0)
    across = lax.broadcasted_iota(jnp.int32, (BLOCK, BLOCK), 1)
    row = lax.broadcasted_iota(jnp.int32, (width, BLOCK), 0)
    eliminate(s_ref, r_ref, base)
    both = r_ref[...]
    inv = jnp.where(up > across, both, 0.0) + jnp.where(up == across, 1.0 / both, 0.0)
    x_ref[here, :] = -full_dot(inv, full_dot(l_ref[here, :], x_ref[...], ((1,), (0,))), ((1,), (0,)))
    x_ref[here, here] = inv
    below = jnp.where(row >= base + BLOCK, full_dot(s_ref[:, here], inv, ((1,), (1,))), 0.0)
    l_ref[:, here] = below
    l_ref[here, here] = jnp.where(up >= across, both.T, 0.0)
    s_ref[...] = s_ref[...] - full_dot(below, below, ((1,), (1,)))


def finish_factor(row_count, col_count, f_ref, e_ref, q_ref, s_ref, l_ref, x_ref):
    width = s_ref.shape[0]
    r = lax.axis_index("row")
    c = lax.axis_index("col")
    per = width // col_count
    rows_dev = width // row_count
    i0 = lax.broadcasted_iota(jnp.int32, (rows_dev, width), 0)
    i1 = lax.broadcasted_iota(jnp.int32, (rows_dev, width), 1)
    pick_rows = jnp.where(i1 == i0 * row_count + r, 1.0, 0.0)
    j0 = lax.broadcasted_iota(jnp.int32, (per, width), 0)
    j1 = lax.broadcasted_iota(jnp.int32, (per, width), 1)
    pick_cols = jnp.where(j1 == j0 * col_count + c, 1.0, 0.0)
    f_ref[...] = full_dot(full_dot(pick_rows, l_ref[...], ((1,), (0,))), pick_cols, ((1,), (1,)))
    natural = lax.broadcasted_iota(jnp.int32, (width, width), 0)
    store = lax.broadcasted_iota(jnp.int32, (width, width), 1)
    from_cols = jnp.where(natural == (store % per) * col_count + store // per, 1.0, 0.0)
    s_ref[...] = full_dot(x_ref[...], from_cols, ((1,), (0,)))
    e_ref[...] = split_rows(full_dot(s_ref[...], pick_cols, ((0,), (1,))))
    q_ref[...] = split_rows(full_dot(s_ref[...], s_ref[...], ((0,), (0,))))


def to_natural(row_count, col_count, g_ref, s_ref, x_ref):
    width = s_ref.shape[0]
    per = width // col_count
    rows_dev = width // row_count
    for r in range(row_count):
        for z in range(col_count):
            s_ref[r * rows_dev : (r + 1) * rows_dev, z * per : (z + 1) * per] = g_ref[r, z]
    natural = lax.broadcasted_iota(jnp.int32, (width, width), 0)
    store = lax.broadcasted_iota(jnp.int32, (width, width), 1)
    from_rows = jnp.where(natural == (store % rows_dev) * row_count + store // rows_dev, 1.0, 0.0)
    from_cols = jnp.where(natural == (store % per) * col_count + store // per, 1.0, 0.0)
    x_ref[...] = one_hot_dot(s_ref[...], from_rows.astype(jnp.bfloat16), 3)
    s_ref[...] = one_hot_dot(x_ref[...].T, from_cols.astype(jnp.bfloat16), 3)


def top_solve(col_count, q_ref, top_ref, t_ref, o_ref):
    groups, length, _ = top_ref.shape
    owners = groups // col_count
    width = q_ref.shape[1]
    for h in range(owners):
        left = jnp.concatenate([top_ref[h * col_count + z] for z in range(col_count)], axis=1)
        solved = split_dot(left, q_ref[...])
        for b in range(width // BLOCK):
            t_ref[b, pl.ds(h, length, stride=owners), :] = solved[:, b * BLOCK : (b + 1) * BLOCK]
    for b in range(width // BLOCK):
        high, low = split(t_ref[b].T)
        at = b * BLOCK
        o_ref[at : at + BLOCK, :] = high
        o_ref[width + at : width + at + BLOCK, :] = high
        o_ref[2 * width + at : 2 * width + at + BLOCK, :] = low


def strip_update(piece_ref, e_ref, t_ref, c_ref, f_ref, at):
    rows = pl.ds(at, STRIP)
    left = jnp.concatenate([piece_ref[z, rows] for z in range(piece_ref.shape[0])], axis=1)
    high, low = split(left)
    left = jnp.concatenate([high, low, high], axis=1)
    dims = (((1,), (0,)), ((), ()))
    f_ref[rows, :] = lax.dot_general(left, e_ref[...], dims, preferred_element_type=jnp.float32)
    c_ref[rows, :] = c_ref[rows, :] - lax.dot_general(left, t_ref[...], dims, preferred_element_type=jnp.float32)


def fetch_pieces(p_ref, buf_ref, piece_ref, sems, part):
    c = lax.axis_index("col")
    for z in range(piece_ref.shape[0]):

        @pl.when(c == z)
        def _():
            pltpu.make_async_copy(p_ref.at[part], piece_ref.at[z], sems.at[z]).start()

        @pl.when(c != z)
        def _():
            pltpu.make_async_copy(buf_ref.at[z, part], piece_ref.at[z], sems.at[z]).start()


def await_pieces(p_ref, piece_ref, sems, part):
    for z in range(piece_ref.shape[0]):
        pltpu.make_async_copy(p_ref.at[part], piece_ref.at[z], sems.at[z]).wait()


def main_kernel(row_count, n, d_ref, p_ref, c_ref, f_ref, e_out, o_out, buf_ref, part_f, part_n, *scratch):
    e_ref, o_ref, trail_ref, piece_ref, solved_ref, trail_in, trail_out, solved_out, piece_sem, keep_sem = scratch[:10]
    scratch = scratch[10:]
    g_ref, top_ref, s_ref, l_ref, x_ref, r_ref, q_ref, t_ref = scratch[:8]
    own_sem, mine_send, mine_recv, col_send, col_recv, row_send, row_recv = scratch[8:15]
    piece_send, piece_recv, line_send, line_recv, fill_sem = scratch[15:]
    r = lax.axis_index("row")
    c = lax.axis_index("col")
    mesh_id = pl.DeviceIdType.MESH
    chunks = line_recv.shape[1]
    length = p_ref.shape[0] // chunks
    top_length = top_ref.shape[1]
    along_col = [(r, lax.rem(c + d, n)) for d in range(1, n)]
    along_row = [(lax.rem(r + d, row_count), c) for d in range(1, row_count)]
    q = lax.rem(r, n)
    swap_row = r - q + c
    barrier = pltpu.get_barrier_semaphore()
    for peer in along_col + along_row:
        pl.semaphore_signal(barrier, inc=1, device_id=peer, device_id_type=mesh_id)

    @pl.when(q != c)
    def _():
        pl.semaphore_signal(barrier, inc=1, device_id=(swap_row, q), device_id_type=mesh_id)
        pl.semaphore_wait(barrier, row_count + n - 1)

    @pl.when(q == c)
    def _():
        pl.semaphore_wait(barrier, row_count + n - 2)

    def remote(src, dst, send, recv, peer):
        return pltpu.make_async_remote_copy(
            src_ref=src, dst_ref=dst, send_sem=send, recv_sem=recv, device_id=peer, device_id_type=mesh_id
        )

    def line(phase, way, k):
        block = c - way * (phase - 1)
        part = pl.ds(pl.multiple_of(k * length, length), length)
        dst = buf_ref.at[block, part]
        src = p_ref.at[part] if phase == 1 else dst
        side = phase * 2 - 2 + (way + 1) // 2
        return remote(src, dst, line_send.at[side, k], line_recv.at[block, k], (r, c + way))

    def spare(where, k):
        return ((where == 0) | (where == n - 1)) & (q == where) & (k * length + length <= top_length)

    def exists(phase, way, k):
        block = c - way * (phase - 1)
        there = (block >= 0) & (block < n)
        return there if phase == 1 else there & jnp.logical_not(spare(c, k))

    def leaves(phase, way, k):
        block = c - way * (phase - 1)
        there = (block >= 0) & (block < n) & (c + way >= 0) & (c + way < n)
        return there & jnp.logical_not(spare(c + way, k))

    def forward(phase, k):
        for way in (1, -1):

            @pl.when(exists(phase, way, k))
            def _():
                line(phase, way, k).wait_recv()

            @pl.when(leaves(phase, way, k))
            def _():
                line(phase, way, k).start()

    own = pltpu.make_async_copy(d_ref, g_ref.at[r, c], own_sem)
    across = [
        remote(d_ref, g_ref.at[r, c], col_send.at[i], col_recv.at[i], peer) for i, peer in enumerate(along_col)
    ]
    for copy in [own] + across:
        copy.start()
    top = p_ref.at[pl.ds(0, top_length)]
    mine = remote(top, top_ref.at[swap_row], mine_send, mine_recv, (swap_row, q))
    keep = pltpu.make_async_copy(top, top_ref.at[r], mine_recv)

    @pl.when(q != c)
    def _():
        mine.start()

    @pl.when(q == c)
    def _():
        keep.start()

    def first(k, carry):
        for way in (1, -1):

            @pl.when(leaves(1, way, k))
            def _():
                line(1, way, k).start()

        return carry

    lax.fori_loop(0, chunks, first, 0)
    done = chunks // 2
    last = chunks - 1

    def span(k):
        return pl.ds(pl.multiple_of(k * length, length), length)

    def load(k):
        return pltpu.make_async_copy(c_ref.at[span(k)], trail_ref.at[k], trail_in.at[k])

    def save(k):
        return (
            pltpu.make_async_copy(trail_ref.at[k], part_n.at[span(k)], trail_out.at[k]),
            pltpu.make_async_copy(solved_ref.at[k], part_f.at[span(k)], solved_out.at[k]),
        )

    for copy in [own] + across:
        copy.wait()
    rows = [
        remote(g_ref.at[r], g_ref.at[r], row_send.at[i], row_recv.at[i], peer) for i, peer in enumerate(along_row)
    ]
    for copy in rows:
        copy.start()

    pieces = [
        remote(top_ref.at[r], top_ref.at[r], piece_send.at[i], piece_recv.at[i], peer)
        for i, peer in enumerate(along_row)
    ]
    for copy in rows:
        copy.wait()
    for k in range(done):
        load(k).start()
    to_natural(row_count, n, g_ref, s_ref, x_ref)
    l_ref[...] = jnp.zeros_like(l_ref)
    x_ref[...] = jnp.zeros_like(x_ref)

    def step(k, carry):
        factor_block(s_ref, l_ref, x_ref, r_ref, pl.multiple_of(k * BLOCK, BLOCK))

        @pl.when(k == 0)
        def _():
            @pl.when(q != c)
            def _():
                mine.wait()

            @pl.when(q == c)
            def _():
                keep.wait()

            for copy in pieces:
                copy.start()
            forward(2, k)

        @pl.when(k < last)
        def _():
            forward(2, k + 1)

        @pl.when(k == last)
        def _():
            forward(3, k - last)

        return carry

    lax.fori_loop(0, chunks, step, 0)
    finish_factor(row_count, n, f_ref, e_ref, q_ref, s_ref, l_ref, x_ref)
    half = chunks // 2

    def soon(k, carry):
        forward(3, k)
        return carry

    lax.fori_loop(1, half, soon, 0)
    for copy in pieces:
        copy.wait()
    spared = top_length // length * length
    ends = (q == c) & ((c == 0) | (c == n - 1))
    fill = []
    if spared:
        fill = [
            pltpu.make_async_copy(
                top_ref.at[r - q + z, pl.ds(0, spared)], buf_ref.at[z, pl.ds(0, spared)], fill_sem.at[z]
            )
            for z in range(n)
        ]

    @pl.when(ends)
    def _():
        for copy in fill:
            copy.start()

    top_solve(n, q_ref, top_ref, t_ref, o_ref)
    keeps = [
        pltpu.make_async_copy(e_ref, e_out, keep_sem.at[0]),
        pltpu.make_async_copy(o_ref, o_out, keep_sem.at[1]),
    ]
    for copy in keeps:
        copy.start()
    for phase in range(3, n):

        def later(k, carry, phase=phase):
            forward(phase, k)
            return carry

        lax.fori_loop(half if phase == 3 else 0, chunks, later, 0)

    @pl.when(ends)
    def _():
        for copy in fill:
            copy.wait()

    def update(k, carry):
        forward(n, k)
        fetch_pieces(p_ref, buf_ref, piece_ref, piece_sem, span(k))
        load(k).wait()
        await_pieces(p_ref, piece_ref, piece_sem, span(k))

        def strip(i, carry):
            at = pl.multiple_of(i * STRIP, STRIP)
            strip_update(piece_ref, e_ref, o_ref, trail_ref.at[k], solved_ref.at[k], at)
            return carry

        lax.fori_loop(0, length // STRIP, strip, 0)
        for copy in save(k):
            copy.start()
        return carry

    lax.fori_loop(0, done, update, 0)
    for k in range(done, chunks):
        forward(n, k)
    for copy in keeps:
        copy.wait()
    for k in range(done):
        for copy in save(k):
            copy.wait()
    for phase in range(1, n):

        def drain(k, carry, phase=phase):
            for way in (1, -1):

                @pl.when(leaves(phase, way, k))
                def _():
                    line(phase, way, k).wait_send()

            return carry

        lax.fori_loop(0, chunks, drain, 0)


def exchange(block, panel, trailing, row_count, n):
    dma = pltpu.SemaphoreType.DMA
    rows, lanes = panel.shape
    columns = trailing.shape[1]
    width = block.shape[0] * row_count
    chunks = width // BLOCK
    length = rows // chunks
    done = chunks // 2
    top_length = columns // (row_count // n)
    square = pltpu.VMEM((width, width), jnp.float32)
    anywhere = pl.BlockSpec(memory_space=pl.ANY)
    vmem = pl.BlockSpec(memory_space=pltpu.VMEM)
    return pl.pallas_call(
        functools.partial(main_kernel, row_count, n),
        out_shape=(
            jax.ShapeDtypeStruct(block.shape, jnp.float32),
            jax.ShapeDtypeStruct((3 * width, lanes), jnp.bfloat16),
            jax.ShapeDtypeStruct((3 * width, columns), jnp.bfloat16),
            jax.ShapeDtypeStruct((n, rows, lanes), jnp.float32),
            jax.ShapeDtypeStruct((done * length, lanes), jnp.float32),
            jax.ShapeDtypeStruct((done * length, columns), jnp.float32),
        ),
        in_specs=[vmem, anywhere, anywhere],
        out_specs=(vmem,) + (anywhere,) * 5,
        scratch_shapes=[
            pltpu.VMEM((3 * width, lanes), jnp.bfloat16),
            pltpu.VMEM((3 * width, columns), jnp.bfloat16),
            pltpu.VMEM((done, length, columns), jnp.float32),
            pltpu.VMEM((n, length, lanes), jnp.float32),
            pltpu.VMEM((done, length, lanes), jnp.float32),
            dma((done,)), dma((done,)), dma((done,)), dma((n,)), dma((2,)),
            pltpu.VMEM((row_count, n) + block.shape, jnp.float32),
            pltpu.VMEM((row_count, top_length, lanes), jnp.float32),
            square, square, square,
            pltpu.VMEM((BLOCK, BLOCK), jnp.float32),
            pltpu.VMEM((3 * width, width), jnp.bfloat16),
            pltpu.VMEM((width // BLOCK, columns, BLOCK), jnp.float32),
            dma, dma, dma, dma((n - 1,)), dma((n - 1,)), dma((row_count - 1,)), dma((row_count - 1,)),
            dma((row_count - 1,)), dma((row_count - 1,)), dma((2 * n, chunks)), dma((n, chunks)),
            dma((n,)),
        ],
        compiler_params=pltpu.CompilerParams(
            collective_id=0, has_side_effects=True, vmem_limit_bytes=60 * 1024 * 1024
        ),
    )(block, panel, trailing)


def closing_kernel(p_ref, buf_ref, e_in, o_in, c_ref, part_f, part_n, d_in, d_out, f_ref, n_ref, *scratch):
    d_ref, e_ref, o_ref, piece_ref, trail_ref, solved_ref, carry_f, carry_n = scratch[:8]
    keep_sem, piece_sem, trail_in, trail_out, solved_out, carry_in, carry_out = scratch[8:]
    strips = carry_n.shape[0]
    length = trail_ref.shape[0]
    start = p_ref.shape[0] - length
    mine = length // STRIP
    copy = pltpu.make_async_copy
    keeps = [copy(e_in, e_ref, keep_sem.at[0]), copy(o_in, o_ref, keep_sem.at[1])]
    whole = [copy(part_f, carry_f, keep_sem.at[2]), copy(carry_f, f_ref.at[pl.ds(0, start)], keep_sem.at[3])]

    factor = [copy(d_in, d_ref, keep_sem.at[4]), copy(d_ref, d_out, keep_sem.at[5])]

    def rows(i):
        return pl.ds(i * STRIP, STRIP)

    loads = [copy(c_ref.at[pl.ds(start + i * STRIP, STRIP)], trail_ref.at[rows(i)], trail_in.at[i]) for i in range(mine)]
    brings = [copy(part_n.at[rows(i)], carry_n.at[i], carry_in.at[i]) for i in range(strips)]
    takes = [copy(carry_n.at[i], n_ref.at[rows(i)], carry_out.at[i]) for i in range(strips)]
    stores = [copy(trail_ref.at[rows(i)], n_ref.at[pl.ds(start + i * STRIP, STRIP)], trail_out.at[i]) for i in range(mine)]
    solved = copy(solved_ref, f_ref.at[pl.ds(start, length)], solved_out)
    part = pl.ds(start, length)
    fetch_pieces(p_ref, buf_ref, piece_ref, piece_sem, part)
    mixed = [item for i in range(mine) for item in brings[strips * i // mine : strips * (i + 1) // mine] + loads[i + 1 : i + 2]]
    for item in keeps + loads[:1] + mixed + whole[:1] + factor[:1]:
        item.start()
    await_pieces(p_ref, piece_ref, piece_sem, part)
    for item in keeps:
        item.wait()
    sent = 0
    for i in range(mine):
        loads[i].wait()
        strip_update(piece_ref, e_ref, o_ref, trail_ref, solved_ref, i * STRIP)
        until = strips * (i + 1) // mine
        for j in range(sent, until):
            brings[j].wait()
            takes[j].start()
        sent = until
        stores[i].start()
    whole[0].wait()
    whole[1].start()
    factor[0].wait()
    factor[1].start()
    solved.start()
    for item in takes + stores + [whole[1], factor[1], solved]:
        item.wait()


def closing(panel, gathered, e_parts, top_parts, trailing, part_f, part_n, factor):
    dma = pltpu.SemaphoreType.DMA
    n, rows, lanes = gathered.shape
    columns = trailing.shape[1]
    start = part_n.shape[0]
    length = rows - start
    anywhere = pl.BlockSpec(memory_space=pl.ANY)
    return pl.pallas_call(
        closing_kernel,
        out_shape=(
            jax.ShapeDtypeStruct(factor.shape, jnp.float32),
            jax.ShapeDtypeStruct((rows, lanes), jnp.float32),
            jax.ShapeDtypeStruct((rows, columns), jnp.float32),
        ),
        in_specs=[anywhere] * 8,
        out_specs=(anywhere,) * 3,
        scratch_shapes=[
            pltpu.VMEM(factor.shape, jnp.float32),
            pltpu.VMEM(e_parts.shape, jnp.bfloat16),
            pltpu.VMEM(top_parts.shape, jnp.bfloat16),
            pltpu.VMEM((n, length, lanes), jnp.float32),
            pltpu.VMEM((length, columns), jnp.float32),
            pltpu.VMEM((length, lanes), jnp.float32),
            pltpu.VMEM((start, lanes), jnp.float32),
            pltpu.VMEM((start // STRIP, STRIP, columns), jnp.float32),
            dma((6,)), dma((n,)), dma((length // STRIP,)), dma((length // STRIP,)), dma,
            dma((start // STRIP,)), dma((start // STRIP,)),
        ],
        compiler_params=pltpu.CompilerParams(vmem_limit_bytes=60 * 1024 * 1024),
    )(panel, gathered, e_parts, top_parts, trailing, part_f, part_n, factor)


def shards(diag_block, panel_below, trailing):
    row_count = lax.axis_size("row")
    n = lax.axis_size("col")
    factor, e_parts, top_parts, gathered, part_f, part_n = exchange(diag_block, panel_below, trailing, row_count, n)
    return tuple(closing(panel_below, gathered, e_parts, top_parts, trailing, part_f, part_n, factor))


def solution(mesh):
    in_specs = (P("row", "col"), P("row", "col"), P("row", "col"))
    out_specs = (P("row", "col"), P("row", "col"), P("row", "col"))
    return jax.shard_map(shards, mesh=mesh, in_specs=in_specs, out_specs=out_specs, check_vma=False)
```
